256 devices in a mesh: qb: 32 (over y, z), kb: 8 (over x, core).
Axes of the slice: x: 4, y: 4, z: 8, core: 2. Of those that a mesh axis runs over, the one named last changes fastest.
Arguments:
- queries: bfloat16 [32, 8, 128, 128], P('qb', 'kb'), may hold values from -64 to 64
- keys: bfloat16 [8, 32, 128, 128], P('kb', 'qb'), may hold values from -6 to 6
- positions: int32 [32768], replicated, may hold values from 0 to 65534, as said below
- tile_mask: int32 [128, 128], P('qb', 'kb'), may hold values from 0 to 1, as said below
- w_query: bfloat16 [1, 128, 128], replicated, may hold values from -0.5 to 0.5
- w_key: bfloat16 [1, 128, 128], replicated, may hold values from -0.5 to 0.5
Outputs:
- row_loss: float32 [32, 8, 128], P('qb', 'kb')
- grad_query: float32 [1, 128, 128], replicated
- grad_key: float32 [1, 128, 128], replicated
The draws below stay inside these ranges and needn't reach their ends.
Inputs may be any that keep to these rules, and one draw needn't show every extreme that they name: `positions`: strictly increasing along the sequence, first 0, last 65534. `tile_mask`: 1 on the diagonal, 0 above it.
All inputs are finite; a program needn't handle non-finite values.
Results may differ from the reference program's by a relative error of at most 0.022.
The reference program's roundings to bfloat16 on the way count: a program that leaves them out, or rounds other values in their place, can miss the bound.
Values may be sent and summed in bfloat16 or wider, within the bound.
No kernel may reach another device: no remote copies, remote signals or barrier semaphores. Data moves between devices by JAX's collectives and lax.ppermute only.
A program may use at most 64 MiB of HBM per device.

```python
import jax
import jax.numpy as jnp
from jax import lax

HEADS = 1
HEAD_DIM = 128
PIECE = 128
SEQ = 32768
NBLOCKS = 128
N_QB = 32
N_KB = 8


def key_base(key):
    picked = jax.random.fold_in(key, 101)
    shape = (SEQ, HEADS * HEAD_DIM)
    values = jnp.clip(jax.random.normal(picked, shape, jnp.float32), -6.0, 6.0)
    return values


def draw_keys(key, part):
    return key_base(key).reshape(N_KB, N_QB, PIECE, HEADS * HEAD_DIM).astype(jnp.bfloat16)


def draw_queries(key, part):
    picked = jax.random.fold_in(key, 202)
    shape = (SEQ, HEADS * HEAD_DIM)
    values = jnp.clip(jax.random.normal(picked, shape, jnp.float32), -6.0, 6.0)
    return values.reshape(N_QB, N_KB, PIECE, HEADS * HEAD_DIM).astype(jnp.bfloat16)


def draw_positions(key, part):
    stride_draw = jax.random.randint(jax.random.fold_in(key, 303), (SEQ,), 1, 3)
    walked = (jnp.cumsum(stride_draw) - stride_draw[0]).astype(jnp.int32)
    last_slot = jnp.arange(SEQ, dtype=jnp.int32) == SEQ - 1
    return jnp.where(last_slot, jnp.int32(2 * SEQ - 2), walked).astype(jnp.int32)


def draw_tile_mask(key, part):
    random_marks = jax.random.randint(jax.random.fold_in(key, 404), (NBLOCKS, NBLOCKS), 0, 4) > 0
    row_ids = jnp.arange(NBLOCKS)[:, None]
    col_ids = jnp.arange(NBLOCKS)[None, :]
    return jnp.where(col_ids < row_ids, random_marks, col_ids == row_ids).astype(jnp.int32)


def scatter_about(own_key, shape, scale, reach, kind=jnp.bfloat16):
    drawn = jax.random.normal(own_key, shape, jnp.float32) * scale
    return jnp.minimum(jnp.maximum(drawn, -reach), reach).astype(kind)


def setup_inputs(seed: int = 0) -> dict:
    seeds = jax.random.split(jax.random.key(seed), 7)
    queries = draw_queries(jax.random.fold_in(seeds[6], 71), 0)
    keys = draw_keys(jax.random.fold_in(seeds[6], 71), 0)
    positions = draw_positions(jax.random.fold_in(seeds[6], 71), 0)
    tile_mask = draw_tile_mask(jax.random.fold_in(seeds[6], 71), 0)
    w_query = scatter_about(seeds[4], (HEADS, HEAD_DIM, HEAD_DIM), HEAD_DIM ** -0.5, 0.5)
    w_key = scatter_about(seeds[5], (HEADS, HEAD_DIM, HEAD_DIM), HEAD_DIM ** -0.5, 0.5)
    return dict(queries=queries, keys=keys, positions=positions, tile_mask=tile_mask, w_query=w_query, w_key=w_key)


NEGATIVE = -1e+30

def rotate(inputs, positions, heads):
    row_count = inputs.shape[0]
    head_width = inputs.shape[1] // heads
    half_width = head_width // 2
    frequency = jnp.exp(jnp.arange(half_width, dtype=jnp.float32) * (-2.0 * jnp.log(jnp.float32(10000.0)) / head_width))
    angles = positions.astype(jnp.float32)[:, None, None] * frequency[None, None, :]
    cosine = jnp.cos(angles)
    sine_vals = jnp.sin(angles)
    shaped = inputs.astype(jnp.float32).reshape(row_count, heads, 2, half_width)
    lower_half = shaped[:, :, 0]
    upper_half = shaped[:, :, 1]
    turned = jnp.stack([lower_half * cosine - upper_half * sine_vals, upper_half * cosine + lower_half * sine_vals], axis=2)
    return turned.reshape(row_count, heads * head_width).astype(jnp.bfloat16)

def feature_map(inputs, weight, heads):
    row_count = inputs.shape[0]
    head_width = weight.shape[1]
    mapped = jnp.einsum('rhd,hde->rhe', inputs.reshape(row_count, heads, head_width).astype(jnp.float32), weight.astype(jnp.float32))
    return (jax.nn.softmax(mapped, axis=-1), jax.nn.softmax(-mapped, axis=-1))

def map_grad(inputs, upper_map, lower_map, dfeature, heads):
    half_width = upper_map.shape[-1]
    dfeat_up = dfeature[..., :half_width]
    dfeat_down = dfeature[..., half_width:]
    dmapped = upper_map * (dfeat_up - lax.optimization_barrier(jnp.sum(upper_map * dfeat_up, -1, keepdims=True))) - lower_map * (dfeat_down - lax.optimization_barrier(jnp.sum(lower_map * dfeat_down, -1, keepdims=True)))
    shaped = inputs.astype(jnp.float32).reshape(inputs.shape[0], heads, half_width)
    return jnp.einsum('rhd,rhe->hde', shaped, dmapped, precision=lax.Precision.HIGHEST)

def reference(queries, keys, positions, tile_mask, w_query, w_key):
    heads = w_query.shape[0]
    head_width = w_query.shape[1]
    seq_total = positions.shape[0]
    query_rot = rotate(queries.reshape(seq_total, -1), positions, heads)
    key_rot = rotate(keys.reshape(seq_total, -1), positions, heads)
    query_up, query_down = feature_map(query_rot, w_query, heads)
    key_up, key_down = feature_map(key_rot, w_key, heads)
    query_features_mapped = jnp.concatenate([query_up, query_down], -1).astype(jnp.bfloat16).astype(jnp.float32)
    key_features_mapped = jnp.concatenate([key_up, key_down], -1).astype(jnp.bfloat16).astype(jnp.float32)
    query_heads = query_rot.reshape(seq_total, heads, head_width).astype(jnp.float32)
    key_heads = key_rot.reshape(seq_total, heads, head_width).astype(jnp.float32)
    block_rows = 512 if seq_total % 512 == 0 else seq_total
    block_count = seq_total // block_rows
    mask_size = tile_mask.shape[0]
    mask_block = seq_total // mask_size
    inv_root = 1.0 / jnp.sqrt(jnp.float32(head_width))

    def one_block(dkey_sum, block_index):
        row_start = (block_index * block_rows).astype(jnp.int32)
        query_part = lax.dynamic_slice_in_dim(query_heads, row_start, block_rows, 0)
        feature_slice = lax.dynamic_slice_in_dim(query_features_mapped, row_start, block_rows, 0)
        pos_part = lax.dynamic_slice_in_dim(positions, row_start, block_rows, 0)
        mask_part = lax.dynamic_slice_in_dim(tile_mask, (row_start // mask_block).astype(jnp.int32), block_rows // mask_block, 0)
        block_ok = jnp.broadcast_to(mask_part[:, None, :, None] > 0, (block_rows // mask_block, mask_block, mask_size, mask_block)).reshape(block_rows, seq_total)
        allowed = (block_ok & (positions[None, :] <= pos_part[:, None]))[None]
        scores = jnp.einsum('qhd,khd->hqk', query_part, key_heads) * inv_root
        student_probs = jnp.einsum('buz,wuz->ubw', feature_slice, key_features_mapped)
        row_top = lax.optimization_barrier(jnp.max(jnp.where(allowed, scores, NEGATIVE), axis=2))
        weights = jnp.where(allowed, jnp.exp(scores - row_top[:, :, None]), 0.0)
        row_total = lax.optimization_barrier(jnp.sum(weights, 2))
        log_sum = lax.optimization_barrier(jnp.sum(weights * jnp.where(allowed, jnp.log(student_probs), 0.0), 2))
        row_norm = lax.optimization_barrier(jnp.sum(jnp.where(allowed, student_probs, 0.0), 2))
        row_loss = lax.optimization_barrier(jnp.sum(jnp.log(row_norm) - log_sum / row_total, 0))
        prob = weights / row_total[:, :, None]
        rounded = (jnp.where(allowed, 1.0 / row_norm[:, :, None] - prob / student_probs, 0.0) / seq_total).astype(jnp.bfloat16)
        pairwise_gradient = lax.optimization_barrier(rounded).astype(jnp.float32)
        query_gradient = jnp.einsum('wes,swm->ewm', pairwise_gradient, key_features_mapped)
        key_gradient = jnp.einsum('lrx,rlv->xlv', pairwise_gradient, feature_slice)
        return (dkey_sum + key_gradient, (row_loss, query_gradient))
    dkey_all, outputs = lax.scan(one_block, jnp.zeros((seq_total, heads, 2 * head_width), jnp.float32), jnp.arange(block_count, dtype=jnp.int32))
    losses = outputs[0].reshape(queries.shape[0], queries.shape[1], queries.shape[2])
    dquery_all = outputs[1].reshape(seq_total, heads, 2 * head_width)
    grad_query = map_grad(query_rot, query_up, query_down, dquery_all, heads)
    grad_key = map_grad(key_rot, key_up, key_down, dkey_all, heads)
    return (losses, grad_query, grad_key)
```

```python
import functools

import jax
import jax.numpy as jnp
from jax import lax
from jax.experimental import pallas as pl
from jax.experimental.pallas import tpu as pltpu
from jax.sharding import Mesh
from jax.sharding import PartitionSpec as P

LOW = -1e30
LOG2E = 1.4426950408889634
LN2 = 0.6931471805599453
TILE = 256
HEAD = 128
FEAT = 256
SLOTS = 40


def rotate(inputs, positions):
    half_width = inputs.shape[1] // 2
    frequency = jnp.exp(
        jnp.arange(half_width, dtype=jnp.float32)
        * (-2.0 * jnp.log(jnp.float32(10000.0)) / inputs.shape[1])
    )
    angles = positions.astype(jnp.float32)[:, None] * frequency[None, :]
    cosine = jnp.cos(angles)
    sine = jnp.sin(angles)
    values = inputs.astype(jnp.float32)
    lower, upper = values[:, :half_width], values[:, half_width:]
    return jnp.concatenate(
        [lower * cosine - upper * sine, upper * cosine + lower * sine], axis=1
    ).astype(jnp.bfloat16)


def send_copies(array, axes):
    copies = jnp.broadcast_to(array, (lax.axis_size(axes), *array.shape))
    return lax.all_to_all(copies, axes, split_axis=0, concat_axis=0, tiled=True)


def nn(a, b):
    return lax.dot_general(a, b, (((1,), (0,)), ((), ())), preferred_element_type=jnp.float32)


def nt(a, b):
    return lax.dot_general(a, b, (((1,), (1,)), ((), ())), preferred_element_type=jnp.float32)


def rows_of(q_ref, stripe):
    return jnp.concatenate([q_ref[2 * stripe, :HEAD], q_ref[2 * stripe + 1, :HEAD]], axis=0)


def features(weight_t, rows):
    mapped = nt(weight_t, rows)
    up = jnp.exp(mapped - jnp.max(mapped, 0, keepdims=True))
    down = jnp.exp(jnp.min(mapped, 0, keepdims=True) - mapped)
    up = up * (1.0 / jnp.sum(up, 0, keepdims=True))
    down = down * (1.0 / jnp.sum(down, 0, keepdims=True))
    return jnp.concatenate([up, down], axis=0)


def turned(a):
    return jnp.transpose(a.astype(jnp.float32)).astype(jnp.bfloat16)


def slot_of(band, stripe, sub):
    return (band * 4 - (band * (band - 1)) // 2 + stripe - band) * 4 + sub


def not_after():
    shape = (TILE, TILE)
    return lax.broadcasted_iota(jnp.int32, shape, 0) <= lax.broadcasted_iota(jnp.int32, shape, 1)


def for_tiles(where, mask, chunk, sub, body):
    x, y, z, c = where[0], where[1], where[2], where[3]
    band = (x - chunk + 4) % 4
    key_tile = band * 32 + c * 16 + y * 4 + sub

    def step(stripe, carry):
        row_tile = stripe * 32 + z * 4 + x
        live = mask[chunk * 16 + stripe * 4 + sub] > 0
        slot = slot_of(band, stripe, sub)

        @pl.when(live & (key_tile < row_tile))
        def _():
            body(stripe, slot, False)

        @pl.when(live & (key_tile == row_tile))
        def _():
            body(stripe, slot, True)

        return carry

    lax.fori_loop(0, 4, step, 0)


def first_kernel(
    where, mask, q_ref, k0, k1, k2, k3, wq_ref, wk_ref,
    stats_ref, top_ref, r_ref, kfeat_ref, qfeat_ref,
    q_turned, qf_low, run, kf_ref,
):
    scale = LOG2E * HEAD**-0.5
    wq_t = turned(wq_ref[...])
    wk_t = turned(wk_ref[...])
    for stripe in range(4):
        rows = rows_of(q_ref, stripe)
        q_turned[stripe] = turned(rows)
        feat = features(wq_t, rows)
        qfeat_ref[stripe] = feat
        qf_low[stripe] = feat.astype(jnp.bfloat16)
    run[0] = jnp.full((4, 8, TILE), LOW, jnp.float32)
    run[1] = jnp.zeros((4, 8, TILE), jnp.float32)
    run[2] = jnp.zeros((4, 8, TILE), jnp.float32)
    run[3] = jnp.zeros((4, 8, TILE), jnp.float32)

    def chunk_tiles(chunk, k_ref):
        def key_step(sub, carry):
            keys = k_ref[pl.ds(pl.multiple_of(sub * TILE, TILE), TILE), :]
            feat = features(wk_t, keys)
            kfeat_ref[chunk * 4 + sub] = feat
            kf_ref[...] = jnp.transpose(feat).astype(jnp.bfloat16)

            def body(stripe, slot, corner):
                raw = nn(keys, q_turned[stripe])
                student = nn(kf_ref[...], qf_low[stripe])
                if corner:
                    ok = not_after()
                    raw = jnp.where(ok, raw, LOW)
                    counted = jnp.where(ok, student, 0.0)
                    student = jnp.where(ok, student, 1.0)
                else:
                    counted = student
                fold = lambda a: a.reshape(TILE // 8, 8, TILE)
                top = jnp.max(jnp.max(fold(raw), 0), 0, keepdims=True) * scale
                t = raw * scale - top
                weight = jnp.exp2(t)
                log_student = jnp.log2(student)
                r_ref[slot] = jnp.exp2(t - log_student)
                total = jnp.sum(fold(weight), 0)
                logs = jnp.sum(fold(weight * log_student), 0)
                norm = jnp.sum(fold(counted), 0)
                top = jnp.broadcast_to(top, (8, TILE))
                top_ref[slot] = top
                old = run[0, stripe]
                new = jnp.maximum(old, top)
                left = jnp.exp2(old - new)
                right = jnp.exp2(top - new)
                run[0, stripe] = new
                run[1, stripe] = run[1, stripe] * left + total * right
                run[2, stripe] = run[2, stripe] * left + logs * right
                run[3, stripe] = run[3, stripe] + norm

            for_tiles(where, mask, chunk, sub, body)
            return carry

        lax.fori_loop(0, 4, key_step, 0)

    for chunk, k_ref in enumerate((k0, k1, k2, k3)):
        chunk_tiles(chunk, k_ref)
    for stripe in range(4):
        lines = [run[0, stripe][:1]] + [
            jnp.sum(run[n, stripe], 0, keepdims=True) for n in (1, 2, 3)
        ]
        for n, line in enumerate(lines):
            for copy in range(8):
                stats_ref[copy, pl.ds(n * 4 + stripe, 1), :] = line


def split3(a):
    high = a.astype(jnp.bfloat16)
    rest = a - high.astype(jnp.float32)
    middle = rest.astype(jnp.bfloat16)
    low = (rest - middle.astype(jnp.float32)).astype(jnp.bfloat16)
    return jnp.concatenate([high, middle, low], axis=0)


def weight_grad(feat, dfeat, rows):
    up, down = feat[:HEAD], feat[HEAD:]
    d1, d2 = dfeat[:HEAD], dfeat[HEAD:]
    dmapped = up * (d1 - jnp.sum(up * d1, 0, keepdims=True)) - down * (
        d2 - jnp.sum(down * d2, 0, keepdims=True)
    )
    parts = nn(split3(dmapped), rows)
    return (parts[2 * HEAD :] + parts[HEAD : 2 * HEAD]) + parts[:HEAD]


def second_kernel(
    where, mask, st_ref, q_ref, k0, k1, k2, k3, top_ref, r_ref, kfeat_ref, qfeat_ref,
    loss_ref, grad_ref,
    lines, losses, qf_low, dq_ref, dk_ref, gq_ref, gk_ref,
):
    top = st_ref[0, 0:4]
    for n in range(1, 8):
        top = jnp.maximum(top, st_ref[n, 0:4])
    total = jnp.zeros_like(top)
    logs = jnp.zeros_like(top)
    norm = jnp.zeros_like(top)
    for n in range(8):
        factor = jnp.exp2(st_ref[n, 0:4] - top)
        total = total + st_ref[n, 4:8] * factor
        logs = logs + st_ref[n, 8:12] * factor
        norm = norm + st_ref[n, 12:16]
    loss = jnp.log(norm) - (logs / total) * LN2
    for stripe in range(4):
        for half in range(2):
            losses[half, stripe] = jnp.broadcast_to(
                loss[stripe : stripe + 1, half * 128 : half * 128 + 128], (8, 128)
            )
    loss_ref[...] = losses[where[3], where[1]][:1]
    base = (1.0 / norm) * (1.0 / 32768.0)
    shift = top + jnp.log2(total) + 15.0
    for stripe in range(4):
        lines[0, stripe] = jnp.broadcast_to(base[stripe : stripe + 1], (8, TILE))
        lines[1, stripe] = jnp.broadcast_to(shift[stripe : stripe + 1], (8, TILE))
        qf_low[stripe] = qfeat_ref[stripe].astype(jnp.bfloat16)
    dq_ref[...] = jnp.zeros_like(dq_ref)
    gk_ref[...] = jnp.zeros_like(gk_ref)

    def chunk_tiles(chunk, k_ref):
        def key_step(sub, carry):
            feat = kfeat_ref[chunk * 4 + sub]
            kf_t = feat.astype(jnp.bfloat16)
            dk_ref[...] = jnp.zeros_like(dk_ref)

            def body(stripe, slot, corner):
                factor = jnp.exp2(top_ref[slot] - lines[1, stripe])
                r = r_ref[slot].reshape(TILE // 8, 8, TILE)
                grad = (lines[0, stripe][None] - r * factor[None]).reshape(TILE, TILE)
                if corner:
                    grad = jnp.where(not_after(), grad, 0.0)
                grad = grad.astype(jnp.bfloat16)
                dq_ref[stripe] += nn(kf_t, grad)
                dk_ref[...] += nt(qf_low[stripe], grad)

            for_tiles(where, mask, chunk, sub, body)
            keys = k_ref[pl.ds(pl.multiple_of(sub * TILE, TILE), TILE), :]
            gk_ref[...] += weight_grad(feat, dk_ref[...], keys)
            return carry

        lax.fori_loop(0, 4, key_step, 0)

    for chunk, k_ref in enumerate((k0, k1, k2, k3)):
        chunk_tiles(chunk, k_ref)
    gq = jnp.zeros((HEAD, HEAD), jnp.float32)
    for stripe in range(4):
        gq = gq + weight_grad(qfeat_ref[stripe], dq_ref[stripe], rows_of(q_ref, stripe))
    grad_ref[0] = jnp.transpose(gq)
    grad_ref[1] = jnp.transpose(gk_ref[...])


def f32(*shape):
    return jax.ShapeDtypeStruct(shape, jnp.float32)


def local(queries, keys, positions, tile_mask, w_query, w_key):
    x, y, z, c = (lax.axis_index(name) for name in ("x", "y", "z", "c"))
    piece = queries.shape[2]
    query_start = ((y * 8 + z) * 8 + x * 2 + c) * piece
    key_start = ((x * 2 + c) * 32 + y * 8 + z) * piece
    own_query = rotate(
        queries.reshape(piece, HEAD), lax.dynamic_slice_in_dim(positions, query_start, piece)
    )
    own_key = rotate(
        keys.reshape(piece, HEAD), lax.dynamic_slice_in_dim(positions, key_start, piece)
    )
    marks = jnp.pad(tile_mask.reshape(1, 64).astype(jnp.bfloat16), ((0, 15), (0, 64)))
    q_all = send_copies(jnp.concatenate([own_query, marks], 0), ("y", "c"))
    k_near = send_copies(own_key, "z").reshape(1024, HEAD)
    marks = jnp.pad(q_all[:, piece], ((0, 8), (0, 0)))
    load = jnp.concatenate([k_near, marks], 0)
    chunks = [load] + [
        lax.ppermute(load, "x", [(i, (i + step) % 4) for i in range(4)]) for step in (1, 2, 3)
    ]
    own = jnp.stack([chunk[1024:1032, :64] for chunk in chunks]).reshape(4, 4, 2, 4, 4, 4)
    own = lax.dynamic_slice(own, (0, 0, c, x, y, 0), (4, 4, 1, 1, 1, 4))
    mask = own.reshape(64).astype(jnp.int32)
    where = jnp.stack([x, y, z, c]).astype(jnp.int32)
    vmem = pl.BlockSpec(memory_space=pltpu.VMEM)
    smem = pl.BlockSpec(memory_space=pltpu.SMEM)
    stats, tops, r, kfeat, qfeat = pl.pallas_call(
        first_kernel,
        out_shape=(
            f32(8, 16, TILE),
            f32(SLOTS, 8, TILE),
            f32(SLOTS, TILE, TILE),
            f32(16, FEAT, TILE),
            f32(4, FEAT, TILE),
        ),
        in_specs=[smem, smem] + [vmem] * 7,
        out_specs=(vmem,) * 5,
        scratch_shapes=[
            pltpu.VMEM((4, HEAD, TILE), jnp.bfloat16),
            pltpu.VMEM((4, FEAT, TILE), jnp.bfloat16),
            pltpu.VMEM((4, 4, 8, TILE), jnp.float32),
            pltpu.VMEM((TILE, FEAT), jnp.bfloat16),
        ],
        name="first",
    )(where, mask, q_all, *chunks, w_query[0], w_key[0])
    stats = lax.all_to_all(stats, ("y", "c"), split_axis=0, concat_axis=0, tiled=True)
    loss, grads = pl.pallas_call(
        second_kernel,
        out_shape=(f32(1, piece), f32(2, HEAD, HEAD)),
        in_specs=[smem, smem] + [vmem] * 10,
        out_specs=(vmem,) * 2,
        scratch_shapes=[
            pltpu.VMEM((2, 4, 8, TILE), jnp.float32),
            pltpu.VMEM((2, 4, 8, 128), jnp.float32),
            pltpu.VMEM((4, FEAT, TILE), jnp.bfloat16),
            pltpu.VMEM((4, FEAT, TILE), jnp.float32),
            pltpu.VMEM((FEAT, TILE), jnp.float32),
            pltpu.VMEM((HEAD, HEAD), jnp.float32),
            pltpu.VMEM((HEAD, HEAD), jnp.float32),
        ],
        name="second",
    )(where, mask, stats, q_all, *chunks, tops, r, kfeat, qfeat)
    wide = ("y", "x", "c")
    part = lax.all_to_all(
        grads.reshape(32, 8, HEAD), wide, split_axis=0, concat_axis=0, tiled=True
    ).sum(0)
    part = send_copies(part, "z").sum(0)
    whole = send_copies(part, wide).reshape(2, 1, HEAD, HEAD)
    return loss.reshape(1, 1, piece), whole[0], whole[1]


def solution(mesh):
    finer = Mesh(mesh.devices.reshape(4, 8, 4, 2), ("y", "z", "x", "c"))
    qb, kb = ("y", "z"), ("x", "c")
    placed = (P(qb, kb, None, None), P(kb, qb, None, None), P(), P(qb, kb), P(), P())
    return jax.shard_map(
        local, mesh=finer, in_specs=placed, out_specs=(P(qb, kb, None), P(), P()), check_vma=False
    )
```

```python
import functools

import jax
import jax.numpy as jnp
from jax import lax
from jax.experimental import pallas as pl
from jax.experimental.pallas import tpu as pltpu
from jax.sharding import Mesh
from jax.sharding import PartitionSpec as P

LOW = -1e30
LOG2E = 1.4426950408889634
LN2 = 0.6931471805599453
TILE = 256
HEAD = 128
FEAT = 256
PIECE = 128
SUB = 64
MARKS = 32
CHUNKS = (0, 1, 3, 2)


def nn(a, b):
    return lax.dot_general(a, b, (((1,), (0,)), ((), ())), preferred_element_type=jnp.float32)


def nt(a, b):
    return lax.dot_general(a, b, (((1,), (1,)), ((), ())), preferred_element_type=jnp.float32)


def fold(a):
    return a.reshape(a.shape[0] // 8, 8, a.shape[1])


def place():
    return tuple(lax.axis_index(name) for name in ("x", "y", "z", "c"))


def rotate_kernel(
    pos_hbm, q_hbm, k_hbm, mask_hbm, wq_hbm, wk_hbm,
    q_out, k_out, wq_out, wk_out,
    lines_ref, values_ref, mask_ref, sems,
):
    x, y, z, c = place()
    pieces = ((y * 8 + z) * 8 + x * 2 + c, (x * 2 + c) * 32 + y * 8 + z)
    copies = [
        pltpu.make_async_copy(pos_hbm.at[pieces[0] // 8], lines_ref.at[0], sems.at[0]),
        pltpu.make_async_copy(pos_hbm.at[pieces[1] // 8], lines_ref.at[1], sems.at[1]),
        pltpu.make_async_copy(q_hbm, values_ref.at[0], sems.at[2]),
        pltpu.make_async_copy(k_hbm, values_ref.at[1], sems.at[3]),
        pltpu.make_async_copy(mask_hbm, mask_ref, sems.at[4]),
        pltpu.make_async_copy(wq_hbm, wq_out, sems.at[5]),
        pltpu.make_async_copy(wk_hbm, wk_out, sems.at[6]),
    ]
    for copy in copies:
        copy.start()
    row = lax.broadcasted_iota(jnp.int32, (8, PIECE), 0)
    base = jnp.ones((8, PIECE), jnp.float32)
    for n in range(1, 8):
        base = jnp.where(row == n, jnp.float32(10000.0 ** (-n / 64)), base)
    frequency = jnp.concatenate(
        [base * jnp.float32(10000.0 ** (-8 * n / 64)) for n in range(8)], 0
    )
    for copy in copies:
        copy.wait()

    def turn(n):
        line = jnp.sum(jnp.where(row == pieces[n] % 8, lines_ref[n], 0), 0, keepdims=True)
        angles = line.astype(jnp.float32) * frequency
        both = jnp.transpose(jnp.concatenate([jnp.cos(angles), jnp.sin(angles)], 0))
        other = pltpu.roll(both, 64, 1)
        low = lax.broadcasted_iota(jnp.int32, (PIECE, HEAD), 1) < 64
        values = values_ref[n].astype(jnp.float32)
        return (
            values * jnp.where(low, both, other)
            + pltpu.roll(values, 64, 1) * jnp.where(low, -other, both)
        ).astype(jnp.bfloat16)

    own_q = turn(0)
    own_k = turn(1)
    marks = mask_ref[...].astype(jnp.float32)
    marks = jnp.concatenate([marks, jnp.zeros((4, 112), jnp.float32)], 1)
    marks = jnp.concatenate([marks, jnp.zeros((12, HEAD), jnp.float32)], 0).astype(jnp.bfloat16)
    q_out[:PIECE] = own_q
    q_out[PIECE:] = marks
    for n in range(8):
        k_out[n] = own_k


def features(weight_t, rows):
    mapped = nt(weight_t, rows)
    up = jnp.exp(mapped - jnp.max(mapped, 0, keepdims=True))
    down = jnp.exp(jnp.min(mapped, 0, keepdims=True) - mapped)
    up = up * (1.0 / jnp.sum(up, 0, keepdims=True))
    down = down * (1.0 / jnp.sum(down, 0, keepdims=True))
    return jnp.concatenate([up, down], axis=0)


def turned(a):
    return jnp.transpose(a.astype(jnp.float32)).astype(jnp.bfloat16)


def not_after(start, count):
    shape = (count, TILE)
    keys = lax.broadcasted_iota(jnp.int32, shape, 0) + start
    return keys <= lax.broadcasted_iota(jnp.int32, shape, 1)


def fetch_marks(k_refs, staged, marks, sems):
    for n, k_ref in enumerate(k_refs):
        staged[n] = k_ref[4 * TILE :, :].astype(jnp.float32).astype(jnp.int32)
        pltpu.make_async_copy(staged.at[n], marks.at[n], sems.at[n]).start()


def wait_marks(k_refs, staged, marks, sems):
    for n in range(len(k_refs)):
        pltpu.make_async_copy(staged.at[n], marks.at[n], sems.at[n]).wait()


def for_tiles(marks, n, chunk, sub, body):
    x, y, z, c = place()
    key_tile = ((x + 4 - chunk) % 4) * 32 + c * 16 + y * 4 + sub

    def step(stripe, carry):
        row_tile = stripe * 32 + z * 4 + x
        back = (y + 4 - stripe) % 4
        live = marks[n, (back ^ (back // 2)) * 8 + x, y * 4 + sub] > 0

        @pl.when(live & (key_tile < row_tile))
        def _():
            body(stripe, False)

        @pl.when(live & (key_tile == row_tile))
        def _():
            body(stripe, True)

        return carry

    lax.fori_loop(0, 4, step, 0)


def first_kernel(chunks, *refs):
    count = len(chunks)
    opens, closes = 0 in chunks, 2 in chunks
    refs = list(refs)
    take = lambda number: [refs.pop(0) for _ in range(number)]
    k_refs = take(count)
    (wk_ref,) = take(1)
    if opens:
        wq_ref, *q_refs = take(5)
        run, q_turned, qf_low, qfeat_ref, rows_ref = take(5)
    else:
        old_run, q_turned, qf_low = take(3)
        (run,) = take(1)
    top_refs, u_refs, kfeat_refs = take(count), take(count), take(count)
    if closes:
        (stats_ref,) = take(1)
    raw_ref, kf_ref, staged, marks, sems = refs
    scale = LOG2E * HEAD**-0.5
    fetch_marks(k_refs, staged, marks, sems)
    wk_t = turned(wk_ref[...])
    if opens:
        wq_t = turned(wq_ref[...])

        x, y, z, c = place()
        for n, q_ref in enumerate(q_refs):
            stripe = (y + 4 - CHUNKS[n]) % 4
            rows_ref[stripe, c] = q_ref[0, :PIECE]
            rows_ref[stripe, 1 - c] = q_ref[1, :PIECE]
        for stripe in range(4):
            rows = rows_ref[stripe].reshape(TILE, HEAD)
            q_turned[stripe] = turned(rows)
            feat = features(wq_t, rows)
            qfeat_ref[stripe] = feat
            qf_low[stripe] = feat.astype(jnp.bfloat16)
        run[0] = jnp.full((4, 8, TILE), LOW, jnp.float32)
        for n in (1, 2, 3):
            run[n] = jnp.zeros((4, 8, TILE), jnp.float32)
    else:
        run[...] = old_run[...]
    wait_marks(k_refs, staged, marks, sems)

    for n, chunk in enumerate(chunks):
        k_ref, top_ref, u_ref, kfeat_ref = k_refs[n], top_refs[n], u_refs[n], kfeat_refs[n]

        def key_step(sub, carry):
            keys = k_ref[pl.ds(pl.multiple_of(sub * TILE, TILE), TILE), :]
            feat = features(wk_t, keys)
            kfeat_ref[sub] = feat
            kf_ref[...] = jnp.transpose(feat.astype(jnp.bfloat16))

            def body(stripe, corner):
                slot = sub * 4 + stripe
                raw = nn(keys, q_turned[stripe])
                if corner:
                    raw = jnp.where(not_after(0, TILE), raw, LOW)
                raw_ref[...] = raw
                top = jnp.max(jnp.max(fold(raw), 0), 0, keepdims=True) * scale
                top = jnp.broadcast_to(top, (8, TILE))
                total = jnp.zeros((8, TILE), jnp.float32)
                logs, norm = total, total
                for start in range(0, TILE, SUB):
                    part = pl.ds(start, SUB)
                    student = nn(kf_ref[part, :], qf_low[stripe])
                    if corner:
                        ok = not_after(start, SUB)
                        norm = norm + jnp.sum(fold(jnp.where(ok, student, 0.0)), 0)
                        student = jnp.where(ok, student, 1.0)
                    else:
                        norm = norm + jnp.sum(fold(student), 0)
                    t = fold(raw_ref[part, :]) * scale - top[None]
                    weight = jnp.exp2(t)
                    log_student = jnp.log2(fold(student))
                    u_ref[slot, part, :] = (t - log_student).reshape(SUB, TILE)
                    total = total + jnp.sum(weight, 0)
                    logs = logs + jnp.sum(weight * log_student, 0)
                top_ref[slot] = top
                old = run[0, stripe]
                new = jnp.maximum(old, top)
                left = jnp.exp2(old - new)
                right = jnp.exp2(top - new)
                run[0, stripe] = new
                run[1, stripe] = run[1, stripe] * left + total * right
                run[2, stripe] = run[2, stripe] * left + logs * right
                run[3, stripe] = run[3, stripe] + norm

            for_tiles(marks, n, chunk, sub, body)
            return carry

        lax.fori_loop(0, 4, key_step, 0)

    if closes:
        lines = [run[0, stripe][:1] for stripe in range(4)] + [
            jnp.sum(run[n, stripe], 0, keepdims=True) for n in (1, 2, 3) for stripe in range(4)
        ]
        lines = jnp.concatenate(lines, 0)
        for copy in range(8):
            stats_ref[copy] = lines


def split2(a):
    high = a.astype(jnp.bfloat16)
    low = (a - high.astype(jnp.float32)).astype(jnp.bfloat16)
    return jnp.concatenate([high, low], axis=0)


def weight_grad(feat, dfeat, rows):
    up, down = feat[:HEAD], feat[HEAD:]
    d1, d2 = dfeat[:HEAD], dfeat[HEAD:]
    dmapped = up * (d1 - jnp.sum(up * d1, 0, keepdims=True)) - down * (
        d2 - jnp.sum(down * d2, 0, keepdims=True)
    )
    parts = nn(split2(dmapped), rows)
    return parts[HEAD:] + parts[:HEAD]


def second_kernel(
    st_ref, q_ref, qfeat_ref, qf_low, *refs
):
    refs = list(refs)
    k_refs, top_refs, u_refs, kfeat_refs = (
        [refs.pop(0) for _ in range(4)] for _ in range(4)
    )
    loss_ref, grad_ref, lines, losses, kf_t, g_ref, dq_ref, dk_ref, gk_ref, staged, marks, sems = refs
    x, y, z, c = place()
    fetch_marks(k_refs, staged, marks, sems)
    top = st_ref[0, 0:4]
    for n in range(1, 8):
        top = jnp.maximum(top, st_ref[n, 0:4])
    total = jnp.zeros_like(top)
    logs = jnp.zeros_like(top)
    norm = jnp.zeros_like(top)
    for n in range(8):
        factor = jnp.exp2(st_ref[n, 0:4] - top)
        total = total + st_ref[n, 4:8] * factor
        logs = logs + st_ref[n, 8:12] * factor
        norm = norm + st_ref[n, 12:16]
    loss = jnp.log(norm) - (logs / total) * LN2
    for stripe in range(4):
        for half in range(2):
            losses[half, stripe] = jnp.broadcast_to(
                loss[stripe : stripe + 1, half * 128 : half * 128 + 128], (8, 128)
            )
    loss_ref[...] = losses[c, y][:1]
    base = (1.0 / norm) * (1.0 / 32768.0)
    shift = top + jnp.log2(total) + 15.0
    for stripe in range(4):
        lines[0, stripe] = jnp.broadcast_to(base[stripe : stripe + 1], (8, TILE))
        lines[1, stripe] = jnp.broadcast_to(shift[stripe : stripe + 1], (8, TILE))
    dq_ref[...] = jnp.zeros_like(dq_ref)
    gk_ref[...] = jnp.zeros_like(gk_ref)
    wait_marks(k_refs, staged, marks, sems)

    for n, chunk in enumerate(CHUNKS):
        k_ref, top_ref, u_ref, kfeat_ref = k_refs[n], top_refs[n], u_refs[n], kfeat_refs[n]

        def key_step(sub, carry):
            kf_t[...] = kfeat_ref[sub].astype(jnp.bfloat16)
            dk_ref[...] = jnp.zeros_like(dk_ref)

            def body(stripe, corner):
                slot = sub * 4 + stripe
                less = lines[1, stripe] - top_ref[slot]
                level = lines[0, stripe]
                for start in range(0, TILE, SUB):
                    part = pl.ds(start, SUB)
                    grad = level[None] - jnp.exp2(fold(u_ref[slot, part, :]) - less[None])
                    grad = grad.reshape(SUB, TILE)
                    if corner:
                        grad = jnp.where(not_after(start, SUB), grad, 0.0)
                    g_ref[part, :] = grad.astype(jnp.bfloat16)
                dq_ref[stripe] += nn(kf_t[...], g_ref[...])
                dk_ref[...] += nt(qf_low[stripe], g_ref[...])

            for_tiles(marks, n, chunk, sub, body)
            keys = k_ref[pl.ds(pl.multiple_of(sub * TILE, TILE), TILE), :]
            gk_ref[...] += weight_grad(kfeat_ref[sub], dk_ref[...], keys)
            return carry

        lax.fori_loop(0, 4, key_step, 0)

    gq = jnp.zeros((HEAD, HEAD), jnp.float32)
    for stripe in range(4):
        gq = gq + weight_grad(qfeat_ref[stripe], dq_ref[stripe], q_ref[stripe].reshape(TILE, HEAD))
    grad_ref[0] = jnp.transpose(gq)
    grad_ref[1] = jnp.transpose(gk_ref[...])


def f32(*shape):
    return jax.ShapeDtypeStruct(shape, jnp.float32)


def b16(*shape):
    return jax.ShapeDtypeStruct(shape, jnp.bfloat16)


def call(kernel, name, outs, scratch, work, *args):
    vmem = pl.BlockSpec(memory_space=pltpu.VMEM)
    return pl.pallas_call(
        kernel,
        out_shape=outs,
        in_specs=[vmem] * len(args),
        out_specs=(vmem,) * len(outs),
        scratch_shapes=scratch,
        compiler_params=pltpu.CompilerParams(vmem_limit_bytes=12 << 20),
        cost_estimate=pl.CostEstimate(
            flops=int(work * 1e8), bytes_accessed=int(work * 1e5), transcendentals=int(work * 1e5)
        ),
        name=name,
    )(*args)


def marks_scratch(count):
    return [
        pltpu.VMEM((count, MARKS, HEAD), jnp.int32),
        pltpu.SMEM((count, MARKS, HEAD), jnp.int32),
        pltpu.SemaphoreType.DMA((count,)),
    ]


def first_call(chunks, loads, w_key, opening, carried):
    count = len(chunks)
    outs = [f32(4, 4, 8, TILE)]
    if opening:
        outs += [b16(4, HEAD, TILE), b16(4, FEAT, TILE), f32(4, FEAT, TILE), b16(4, 2, PIECE, HEAD)]
    outs += [f32(16, 8, TILE)] * count + [f32(16, TILE, TILE)] * count
    outs += [f32(4, FEAT, TILE)] * count
    if 2 in chunks:
        outs += [f32(8, 16, TILE)]
    scratch = [
        pltpu.VMEM((TILE, TILE), jnp.float32),
        pltpu.VMEM((TILE, FEAT), jnp.bfloat16),
    ] + marks_scratch(count)
    return call(
        functools.partial(first_kernel, chunks),
        "first%d" % chunks[0],
        tuple(outs),
        scratch,
        20 * count,
        *loads,
        w_key,
        *(opening or carried),
    )


def exchanged(copies, axes):
    return lax.all_to_all(copies, axes, split_axis=0, concat_axis=0, tiled=True)


def local(queries, keys, positions, tile_mask, w_query, w_key):
    hbm = pl.BlockSpec(memory_space=pltpu.HBM)
    vmem = pl.BlockSpec(memory_space=pltpu.VMEM)
    q_own, k_copies, w_query, w_key = pl.pallas_call(
        rotate_kernel,
        out_shape=(
            b16(PIECE + 16, HEAD), b16(8, PIECE, HEAD), b16(HEAD, HEAD), b16(HEAD, HEAD)
        ),
        in_specs=[hbm] * 6,
        out_specs=(vmem,) * 4,
        scratch_shapes=[
            pltpu.VMEM((2, 8, PIECE), jnp.int32),
            pltpu.VMEM((2, PIECE, HEAD), jnp.bfloat16),
            pltpu.VMEM((4, 16), jnp.int32),
            pltpu.SemaphoreType.DMA((7,)),
        ],
        compiler_params=pltpu.CompilerParams(vmem_limit_bytes=60 << 20),
        name="rotate",
    )(
        positions.reshape(32, 8, PIECE),
        queries.reshape(PIECE, HEAD),
        keys.reshape(PIECE, HEAD),
        tile_mask,
        w_query[0],
        w_key[0],
    )
    k_near = exchanged(k_copies, "z")
    other = lax.ppermute(q_own, "c", [(0, 1), (1, 0)])
    pair = jnp.stack([q_own, other])
    pairs = [pair] + [
        lax.ppermute(pair, "y", [(i, (i + step) % 4) for i in range(4)]) for step in (1, 3, 2)
    ]
    marks = jnp.stack([near[:, PIECE : PIECE + 4] for near in pairs]).reshape(MARKS, HEAD)
    load = jnp.concatenate([k_near.reshape(4 * TILE, HEAD), marks], 0)
    loads = {0: load}
    for step in (1, 3, 2):
        loads[step] = lax.ppermute(load, "x", [(i, (i + step) % 4) for i in range(4)])
    run, q_turned, qf_low, qfeat, q_rows, *rest = first_call(
        (0,), [load], w_key, (w_query, *pairs), ()
    )
    tops, us, kfeats = ([item] for item in rest)
    for chunks in ((1, 3), (2,)):
        run, *rest = first_call(
            chunks, [loads[n] for n in chunks], w_key, (), (run, q_turned, qf_low)
        )
        count = len(chunks)
        tops += rest[:count]
        us += rest[count : 2 * count]
        kfeats += rest[2 * count : 3 * count]
    stats = exchanged(rest[-1], ("y", "c"))
    loss, grads = call(
        second_kernel,
        "second",
        (f32(1, PIECE), f32(2, HEAD, HEAD)),
        [
            pltpu.VMEM((2, 4, 8, TILE), jnp.float32),
            pltpu.VMEM((2, 4, 8, 128), jnp.float32),
            pltpu.VMEM((FEAT, TILE), jnp.bfloat16),
            pltpu.VMEM((TILE, TILE), jnp.bfloat16),
            pltpu.VMEM((4, FEAT, TILE), jnp.float32),
            pltpu.VMEM((FEAT, TILE), jnp.float32),
            pltpu.VMEM((HEAD, HEAD), jnp.float32),
        ]
        + marks_scratch(4),
        100,
        stats,
        q_rows,
        qfeat,
        qf_low,
        *[loads[n] for n in CHUNKS],
        *tops,
        *us,
        *kfeats,
    )
    wide = ("y", "x", "c")
    part = exchanged(grads.reshape(32, 8, HEAD), wide).sum(0)
    part = exchanged(jnp.broadcast_to(part, (8, 8, HEAD)), "z").sum(0)
    whole = exchanged(jnp.broadcast_to(part, (32, 8, HEAD)), wide).reshape(2, 1, HEAD, HEAD)
    return loss.reshape(1, 1, PIECE), whole[0], whole[1]


def solution(mesh):
    finer = Mesh(mesh.devices.reshape(4, 8, 4, 2), ("y", "z", "x", "c"))
    qb, kb = ("y", "z"), ("x", "c")
    placed = (P(qb, kb, None, None), P(kb, qb, None, None), P(), P(qb, kb), P(), P())
    return jax.shard_map(
        local, mesh=finer, in_specs=placed, out_specs=(P(qb, kb, None), P(), P()), check_vma=False
    )
```

```python
import functools

import jax
import jax.numpy as jnp
from jax import lax
from jax.experimental import pallas as pl
from jax.experimental.pallas import tpu as pltpu
from jax.sharding import Mesh
from jax.sharding import PartitionSpec as P

LOW = -1e30
LOG2E = 1.4426950408889634
LN2 = 0.6931471805599453
TILE = 256
HEAD = 128
FEAT = 256
PIECE = 128
MARK_ROW = 512
LISTED = 64
GROUPS = ((0,), (1, 3), (2,))
MARKS = 32
CHUNKS = (0, 1, 3, 2)


def nn(a, b):
    return lax.dot_general(a, b, (((1,), (0,)), ((), ())), preferred_element_type=jnp.float32)


def nt(a, b):
    return lax.dot_general(a, b, (((1,), (1,)), ((), ())), preferred_element_type=jnp.float32)


def fold(a):
    return a.reshape(a.shape[0] // 8, 8, a.shape[1])


def place():
    return tuple(lax.axis_index(name) for name in ("x", "y", "z", "c"))


def rotate_kernel(
    pos_hbm, q_hbm, k_hbm, mask_hbm, wq_hbm, wk_hbm,
    q_out, k_out, wq_out, wk_out,
    lines_ref, values_ref, mask_ref, sems,
):
    x, y, z, c = place()
    pieces = ((y * 8 + z) * 8 + x * 2 + c, (x * 2 + c) * 32 + y * 8 + z)
    copies = [
        pltpu.make_async_copy(pos_hbm.at[pieces[0] // 8], lines_ref.at[0], sems.at[0]),
        pltpu.make_async_copy(pos_hbm.at[pieces[1] // 8], lines_ref.at[1], sems.at[1]),
        pltpu.make_async_copy(q_hbm, values_ref.at[0], sems.at[2]),
        pltpu.make_async_copy(k_hbm, values_ref.at[1], sems.at[3]),
        pltpu.make_async_copy(mask_hbm, mask_ref, sems.at[4]),
        pltpu.make_async_copy(wq_hbm, wq_out, sems.at[5]),
        pltpu.make_async_copy(wk_hbm, wk_out, sems.at[6]),
    ]
    for copy in copies:
        copy.start()
    row = lax.broadcasted_iota(jnp.int32, (8, PIECE), 0)
    base = jnp.ones((8, PIECE), jnp.float32)
    for n in range(1, 8):
        base = jnp.where(row == n, jnp.float32(10000.0 ** (-n / 64)), base)
    frequency = jnp.concatenate(
        [base * jnp.float32(10000.0 ** (-8 * n / 64)) for n in range(8)], 0
    )
    for copy in copies:
        copy.wait()

    def turn(n):
        line = jnp.sum(jnp.where(row == pieces[n] % 8, lines_ref[n], 0), 0, keepdims=True)
        angles = line.astype(jnp.float32) * frequency
        both = jnp.transpose(jnp.concatenate([jnp.cos(angles), jnp.sin(angles)], 0))
        other = pltpu.roll(both, 64, 1)
        low = lax.broadcasted_iota(jnp.int32, (PIECE, HEAD), 1) < 64
        values = values_ref[n].astype(jnp.float32)
        return (
            values * jnp.where(low, both, other)
            + pltpu.roll(values, 64, 1) * jnp.where(low, -other, both)
        ).astype(jnp.bfloat16)

    own_q = turn(0)
    own_k = turn(1)
    marks = mask_ref[...].astype(jnp.float32)
    marks = jnp.concatenate([marks, jnp.zeros((4, 112), jnp.float32)], 1)
    marks = jnp.concatenate([marks, jnp.zeros((12, HEAD), jnp.float32)], 0).astype(jnp.bfloat16)
    q_out[:PIECE] = own_q
    q_out[PIECE:] = marks
    for n in range(8):
        k_out[n] = own_k


def features(weight_t, rows):
    mapped = nt(weight_t, rows)
    up = jnp.exp(mapped - jnp.max(mapped, 0, keepdims=True))
    down = jnp.exp(jnp.min(mapped, 0, keepdims=True) - mapped)
    up = up * (1.0 / jnp.sum(up, 0, keepdims=True))
    down = down * (1.0 / jnp.sum(down, 0, keepdims=True))
    return jnp.concatenate([up, down], axis=0)


def turned(a):
    return jnp.transpose(a.astype(jnp.float32)).astype(jnp.bfloat16)


def not_after():
    shape = (TILE, TILE)
    return lax.broadcasted_iota(jnp.int32, shape, 0) <= lax.broadcasted_iota(jnp.int32, shape, 1)


def listed(marks, chunks, full, corner):
    x, y, z, c = place()
    spare = len(chunks) * 16
    counts = [jnp.int32(0), jnp.int32(0)]
    for n, chunk in enumerate(chunks):
        first_tile = ((x + 4 - chunk) % 4) * 32 + c * 16 + y * 4
        for stripe in range(4):
            row_tile = stripe * 32 + z * 4 + x
            back = (y + 4 - stripe) % 4
            row = (back ^ (back // 2)) * 8 + x
            for sub in range(4):
                live = marks[n, row, y * 4 + sub] > 0
                kinds = (first_tile + sub < row_tile, first_tile + sub == row_tile)
                for which, (kind, tiles) in enumerate(zip(kinds, (full, corner))):
                    tiles[counts[which]] = (n * 4 + sub) * 4 + stripe
                    counts[which] = counts[which] + (live & kind).astype(jnp.int32)
    for count, tiles in zip(counts, (full, corner)):
        for n in range(3):
            tiles[count + n] = spare
        tiles[LISTED - 1] = count


def in_pairs(tiles, begin, finish, zero):
    count = tiles[LISTED - 1]

    def pair(n, ahead):
        here, there, after = (tiles[2 * n + step] for step in range(3))
        other = begin(there, 1)
        finish(here, 0, ahead)
        ahead = begin(after, 0)
        finish(there, 1, other)
        return ahead

    lax.fori_loop(0, (count + 1) // 2, pair, begin(tiles[0], 0))


def first_kernel(chunks, *refs):
    count = len(chunks)
    opens, closes = 0 in chunks, 2 in chunks
    spare = count * 16
    refs = list(refs)
    take = lambda number: [refs.pop(0) for _ in range(number)]
    k_refs = take(count + closes)
    (wk_ref,) = take(1)
    if opens:
        wq_ref, *q_refs = take(5)
    else:
        old_run, q_turned, qf_low = take(3)
    run, top_ref, u_ref, kfeat_ref, kft_ref, keys_ref, full, corner = take(8)
    if opens:
        q_turned, qf_low, qfeat_ref, rows_ref, dk_ref, dq_ref = take(6)
    if closes:
        (stats_ref,) = take(1)
    raw_a, raw_b, kf_ref, staged, marks, sems = refs
    scale = LOG2E * HEAD**-0.5
    x, y, z, c = place()
    fetched = []
    for n in range(count):
        staged[n] = k_refs[n][MARK_ROW : MARK_ROW + MARKS, :].astype(jnp.float32).astype(jnp.int32)
        fetched.append(pltpu.make_async_copy(staged.at[n], marks.at[n], sems.at[n]))
        fetched[-1].start()
    wk_t = turned(wk_ref[...])
    if opens:
        wq_t = turned(wq_ref[...])
        for n, q_ref in enumerate(q_refs):
            stripe = (y + 4 - CHUNKS[n]) % 4
            rows_ref[stripe, c] = q_ref[0, :PIECE]
            rows_ref[stripe, 1 - c] = q_ref[1, :PIECE]
        for stripe in range(4):
            rows = rows_ref[stripe].reshape(TILE, HEAD)
            q_turned[stripe] = turned(rows)
            feat = features(wq_t, rows)
            qfeat_ref[stripe] = feat
            qf_low[stripe] = feat.astype(jnp.bfloat16)
        run[0] = jnp.full((5, 8, TILE), LOW, jnp.float32)
        for n in (1, 2, 3):
            run[n] = jnp.zeros((5, 8, TILE), jnp.float32)
        for n in range(17):
            dk_ref[n] = jnp.zeros((FEAT, TILE), jnp.float32)
        for n in range(5):
            dq_ref[n] = jnp.zeros((FEAT, TILE), jnp.float32)
    else:
        run[...] = old_run[...]

    for n in range(count):
        for sub in range(4):
            if closes and chunks[n] == 2 and sub >= 2:
                keys = k_refs[n + 1][(sub - 2) * TILE : (sub - 1) * TILE, :]
            else:
                start = sub * TILE + (MARKS if sub >= 2 else 0)
                keys = k_refs[n][start : start + TILE, :]
            keys_ref[n * 4 + sub] = keys
            feat = features(wk_t, keys)
            kfeat_ref[n * 4 + sub] = feat
            low = feat.astype(jnp.bfloat16)
            kft_ref[n * 4 + sub] = low
            kf_ref[n * 4 + sub] = jnp.transpose(low)
    for copy in fetched:
        copy.wait()
    listed(marks, chunks, full, corner)

    def begin(tile, side, cut=False):
        raw = nn(keys_ref[tile // 4], q_turned[tile % 4])
        if cut:
            raw = jnp.where(not_after(), raw, LOW)
        (raw_b if side else raw_a)[...] = raw
        top = jnp.max(jnp.max(fold(raw), 0), 0, keepdims=True) * scale
        return jnp.broadcast_to(top, (8, TILE))

    def finish(tile, side, top, cut=False):
        student = nn(kf_ref[tile // 4], qf_low[tile % 4])
        if cut:
            norm = jnp.sum(fold(jnp.where(not_after(), student, 0.0)), 0)
            student = jnp.where(not_after(), student, 1.0)
        else:
            norm = jnp.sum(fold(student), 0)
        t = fold((raw_b if side else raw_a)[...]) * scale - top[None]
        weight = jnp.exp2(t)
        log_student = jnp.log2(fold(student))
        u_ref[tile] = (t - log_student).reshape(TILE, TILE)
        total = jnp.sum(weight, 0)
        logs = jnp.sum(weight * log_student, 0)
        top_ref[tile] = top
        stripe = jnp.where(tile == spare, 4, tile % 4)
        old = run[0, stripe]
        new = jnp.maximum(old, top)
        left = jnp.exp2(old - new)
        right = jnp.exp2(top - new)
        run[0, stripe] = new
        run[1, stripe] = run[1, stripe] * left + total * right
        run[2, stripe] = run[2, stripe] * left + logs * right
        run[3, stripe] = run[3, stripe] + norm

    in_pairs(full, begin, finish, None)

    def corner_step(n, carry):
        tile = corner[n]
        finish(tile, 0, begin(tile, 0, True), True)
        return carry

    lax.fori_loop(0, corner[LISTED - 1], corner_step, 0)

    if closes:
        lines = [run[0, stripe][:1] for stripe in range(4)] + [
            jnp.sum(run[n, stripe], 0, keepdims=True) for n in (1, 2, 3) for stripe in range(4)
        ]
        lines = jnp.concatenate(lines, 0)
        for copy in range(8):
            stats_ref[copy] = lines


def split2(a):
    high = a.astype(jnp.bfloat16)
    low = (a - high.astype(jnp.float32)).astype(jnp.bfloat16)
    return jnp.concatenate([high, low], axis=0)


def weight_grad(feat, dfeat, rows):
    up, down = feat[:HEAD], feat[HEAD:]
    d1, d2 = dfeat[:HEAD], dfeat[HEAD:]
    dmapped = up * (d1 - jnp.sum(up * d1, 0, keepdims=True)) - down * (
        d2 - jnp.sum(down * d2, 0, keepdims=True)
    )
    parts = nn(split2(dmapped), rows)
    return parts[HEAD:] + parts[:HEAD]


def second_kernel(st_ref, q_ref, qfeat_ref, qf_low, dk_in, dq_in, *refs):
    refs = list(refs)
    groups = [[refs.pop(0) for _ in range(7)] for _ in GROUPS]
    loss_ref, grad_ref, dk_ref, dq_ref, lines, losses, g_a, g_b = refs
    x, y, z, c = place()
    top = st_ref[0, 0:4]
    for n in range(1, 8):
        top = jnp.maximum(top, st_ref[n, 0:4])
    total = jnp.zeros_like(top)
    logs = jnp.zeros_like(top)
    norm = jnp.zeros_like(top)
    for n in range(8):
        factor = jnp.exp2(st_ref[n, 0:4] - top)
        total = total + st_ref[n, 4:8] * factor
        logs = logs + st_ref[n, 8:12] * factor
        norm = norm + st_ref[n, 12:16]
    loss = jnp.log(norm) - (logs / total) * LN2
    for stripe in range(4):
        for half in range(2):
            losses[half, stripe] = jnp.broadcast_to(
                loss[stripe : stripe + 1, half * 128 : half * 128 + 128], (8, 128)
            )
    loss_ref[...] = losses[c, y][:1]
    base = (1.0 / norm) * (1.0 / 32768.0)
    shift = top + jnp.log2(total) + 15.0
    for stripe in range(4):
        lines[0, stripe] = jnp.broadcast_to(base[stripe : stripe + 1], (8, TILE))
        lines[1, stripe] = jnp.broadcast_to(shift[stripe : stripe + 1], (8, TILE))

    gk = jnp.zeros((HEAD, HEAD), jnp.float32)
    offset = 0
    for chunks, group in zip(GROUPS, groups):
        top_ref, u_ref, kfeat_ref, kft_ref, keys_ref, full, corner = group
        spare = 16 * len(chunks)

        def begin(tile, side, cut=False):
            stripe = tile % 4
            less = lines[1, stripe] - top_ref[tile]
            grad = lines[0, stripe][None] - jnp.exp2(fold(u_ref[tile]) - less[None])
            grad = grad.reshape(TILE, TILE)
            if cut:
                grad = jnp.where(not_after(), grad, 0.0)
            (g_b if side else g_a)[...] = grad.astype(jnp.bfloat16)
            return 0

        def finish(tile, side, ahead):
            grad = (g_b if side else g_a)[...]
            key_tile = jnp.where(tile == spare, 16, offset + tile // 4)
            stripe = jnp.where(tile == spare, 4, tile % 4)
            dq_ref[stripe] += nn(kft_ref[tile // 4], grad)
            dk_ref[key_tile] += nt(qf_low[tile % 4], grad)

        in_pairs(full, begin, finish, None)

        def corner_step(n, carry):
            tile = corner[n]
            begin(tile, 0, True)
            finish(tile, 0, 0)
            return carry

        lax.fori_loop(0, corner[LISTED - 1], corner_step, 0)
        for key_tile in range(4 * len(chunks)):
            gk = gk + weight_grad(
                kfeat_ref[key_tile], dk_ref[offset + key_tile], keys_ref[key_tile]
            )
        offset += 4 * len(chunks)

    gq = jnp.zeros((HEAD, HEAD), jnp.float32)
    for stripe in range(4):
        gq = gq + weight_grad(
            qfeat_ref[stripe], dq_ref[stripe], q_ref[stripe].reshape(TILE, HEAD)
        )
    grad_ref[0] = jnp.transpose(gq)
    grad_ref[1] = jnp.transpose(gk)


def f32(*shape):
    return jax.ShapeDtypeStruct(shape, jnp.float32)


def b16(*shape):
    return jax.ShapeDtypeStruct(shape, jnp.bfloat16)


def params(work, limit=12):
    return dict(
        compiler_params=pltpu.CompilerParams(vmem_limit_bytes=limit << 20),
        cost_estimate=pl.CostEstimate(
            flops=int(work * 1e8), bytes_accessed=int(work * 1e5), transcendentals=int(work * 1e5)
        ),
    )


VMEM = pl.BlockSpec(memory_space=pltpu.VMEM)
SMEM = pl.BlockSpec(memory_space=pltpu.SMEM)


def first_call(chunks, loads, w_key, *others):
    count = len(chunks)
    outs = [
        f32(4, 5, 8, TILE),
        f32(16 * count + 1, 8, TILE),
        f32(16 * count + 1, TILE, TILE),
        f32(4 * count, FEAT, TILE),
        b16(4 * count + 1, FEAT, TILE),
        b16(4 * count + 1, TILE, HEAD),
        jax.ShapeDtypeStruct((LISTED,), jnp.int32),
        jax.ShapeDtypeStruct((LISTED,), jnp.int32),
    ]
    if 0 in chunks:
        outs += [
            b16(4, HEAD, TILE),
            b16(4, FEAT, TILE),
            f32(4, FEAT, TILE),
            b16(4, 2, PIECE, HEAD),
            f32(17, FEAT, TILE),
            f32(5, FEAT, TILE),
        ]
    if 2 in chunks:
        outs += [f32(8, 16, TILE)]
    return pl.pallas_call(
        functools.partial(first_kernel, chunks),
        out_shape=tuple(outs),
        in_specs=[VMEM] * (len(loads) + 1 + len(others)),
        out_specs=tuple(SMEM if n in (6, 7) else VMEM for n in range(len(outs))),
        scratch_shapes=[
            pltpu.VMEM((TILE, TILE), jnp.float32),
            pltpu.VMEM((TILE, TILE), jnp.float32),
            pltpu.VMEM((4 * count + 1, TILE, FEAT), jnp.bfloat16),
            pltpu.VMEM((count, MARKS, HEAD), jnp.int32),
            pltpu.SMEM((count, MARKS, HEAD), jnp.int32),
            pltpu.SemaphoreType.DMA((count,)),
        ],
        name="first%d" % chunks[0],
        **params(20 * count),
    )(*loads, w_key, *others)


def exchanged(copies, axes):
    return lax.all_to_all(copies, axes, split_axis=0, concat_axis=0, tiled=True)


def local(queries, keys, positions, tile_mask, w_query, w_key):
    hbm = pl.BlockSpec(memory_space=pltpu.HBM)
    vmem = pl.BlockSpec(memory_space=pltpu.VMEM)
    q_own, k_copies, w_query, w_key = pl.pallas_call(
        rotate_kernel,
        out_shape=(
            b16(PIECE + 16, HEAD), b16(8, PIECE, HEAD), b16(HEAD, HEAD), b16(HEAD, HEAD)
        ),
        in_specs=[hbm] * 6,
        out_specs=(vmem,) * 4,
        scratch_shapes=[
            pltpu.VMEM((2, 8, PIECE), jnp.int32),
            pltpu.VMEM((2, PIECE, HEAD), jnp.bfloat16),
            pltpu.VMEM((4, 16), jnp.int32),
            pltpu.SemaphoreType.DMA((7,)),
        ],
        compiler_params=pltpu.CompilerParams(vmem_limit_bytes=60 << 20),
        name="rotate",
    )(
        positions.reshape(32, 8, PIECE),
        queries.reshape(PIECE, HEAD),
        keys.reshape(PIECE, HEAD),
        tile_mask,
        w_query[0],
        w_key[0],
    )
    k_near = exchanged(k_copies, "z").reshape(4 * TILE, HEAD)
    other = lax.ppermute(q_own, "c", [(0, 1), (1, 0)])
    pair = jnp.stack([q_own, other])
    pairs = [pair] + [
        lax.ppermute(pair, "y", [(i, (i + step) % 4) for i in range(4)]) for step in (1, 3, 2)
    ]
    marks = jnp.stack([near[:, PIECE : PIECE + 4] for near in pairs]).reshape(MARKS, HEAD)
    half = 2 * TILE
    load = jnp.concatenate([k_near[:half], marks, k_near[half:]], 0)
    after = [(i, (i + 1) % 4) for i in range(4)]
    before = [(i, (i + 3) % 4) for i in range(4)]
    lower = lax.ppermute(load, "x", after)
    upper = lax.ppermute(load, "x", before)
    far = (
        lax.ppermute(lower[: half + MARKS], "x", after),
        lax.ppermute(upper[half + MARKS :], "x", before),
    )
    run, *first, q_turned, qf_low, qfeat, q_rows, dk, dq = first_call(
        (0,), [load], w_key, w_query, *pairs
    )
    run, *second = first_call((1, 3), [lower, upper], w_key, run, q_turned, qf_low)
    run, *third, stats = first_call((2,), far, w_key, run, q_turned, qf_low)
    stats = exchanged(stats, ("y", "c"))
    loss, grads, _, _ = pl.pallas_call(
        second_kernel,
        out_shape=(f32(1, PIECE), f32(2, HEAD, HEAD), f32(17, FEAT, TILE), f32(5, FEAT, TILE)),
        in_specs=[VMEM] * 6 + ([VMEM] * 5 + [SMEM] * 2) * 3,
        out_specs=(VMEM,) * 4,
        scratch_shapes=[
            pltpu.VMEM((2, 4, 8, TILE), jnp.float32),
            pltpu.VMEM((2, 4, 8, 128), jnp.float32),
            pltpu.VMEM((TILE, TILE), jnp.bfloat16),
            pltpu.VMEM((TILE, TILE), jnp.bfloat16),
        ],
        input_output_aliases={4: 2, 5: 3},
        name="second",
        **params(100),
    )(stats, q_rows, qfeat, qf_low, dk, dq, *first, *second, *third)
    wide = ("y", "x", "c")
    part = exchanged(grads.reshape(32, 8, HEAD), wide).sum(0)
    part = exchanged(jnp.broadcast_to(part, (8, 8, HEAD)), "z").sum(0)
    whole = exchanged(jnp.broadcast_to(part, (32, 8, HEAD)), wide).reshape(2, 1, HEAD, HEAD)
    return loss.reshape(1, 1, PIECE), whole[0], whole[1]


def solution(mesh):
    finer = Mesh(mesh.devices.reshape(4, 8, 4, 2), ("y", "z", "x", "c"))
    qb, kb = ("y", "z"), ("x", "c")
    placed = (P(qb, kb, None, None), P(kb, qb, None, None), P(), P(qb, kb), P(), P())
    return jax.shard_map(
        local, mesh=finer, in_specs=placed, out_specs=(P(qb, kb, None), P(), P()), check_vma=False
    )
```

```python
import functools

import jax
import jax.numpy as jnp
from jax import lax
from jax.experimental import pallas as pl
from jax.experimental.pallas import tpu as pltpu
from jax.sharding import Mesh
from jax.sharding import PartitionSpec as P

LOW = -1e30
LOG2E = 1.4426950408889634
LN2 = 0.6931471805599453
TILE = 256
HEAD = 128
FEAT = 256
PIECE = 128
MARK_ROW = 512
LISTED = 96
SPARE = 64
WIDTH = 4
GROUPS = ((0,), (1, 3), (2,))
MARKS = 32
CHUNKS = (0, 1, 3, 2)


def nn(a, b):
    return lax.dot_general(a, b, (((1,), (0,)), ((), ())), preferred_element_type=jnp.float32)


def nt(a, b):
    return lax.dot_general(a, b, (((1,), (1,)), ((), ())), preferred_element_type=jnp.float32)


def fold(a):
    return a.reshape(a.shape[0] // 8, 8, a.shape[1])


def place():
    return tuple(lax.axis_index(name) for name in ("x", "y", "z", "c"))


def rotate_kernel(
    pos_hbm, q_hbm, k_hbm, mask_hbm,
    q_out, k_out,
    lines_ref, values_ref, mask_ref, sems,
):
    x, y, z, c = place()
    pieces = ((y * 8 + z) * 8 + x * 2 + c, (x * 2 + c) * 32 + y * 8 + z)
    copies = [
        pltpu.make_async_copy(pos_hbm.at[pieces[0] // 8], lines_ref.at[0], sems.at[0]),
        pltpu.make_async_copy(pos_hbm.at[pieces[1] // 8], lines_ref.at[1], sems.at[1]),
        pltpu.make_async_copy(q_hbm, values_ref.at[0], sems.at[2]),
        pltpu.make_async_copy(k_hbm, values_ref.at[1], sems.at[3]),
        pltpu.make_async_copy(mask_hbm, mask_ref, sems.at[4]),
    ]
    for copy in copies:
        copy.start()
    row = lax.broadcasted_iota(jnp.int32, (8, PIECE), 0)
    base = jnp.ones((8, PIECE), jnp.float32)
    for n in range(1, 8):
        base = jnp.where(row == n, jnp.float32(10000.0 ** (-n / 64)), base)
    frequency = jnp.concatenate(
        [base * jnp.float32(10000.0 ** (-8 * n / 64)) for n in range(8)], 0
    )
    for copy in copies:
        copy.wait()

    def turn(n):
        line = jnp.sum(jnp.where(row == pieces[n] % 8, lines_ref[n], 0), 0, keepdims=True)
        angles = line.astype(jnp.float32) * frequency
        both = jnp.transpose(jnp.concatenate([jnp.cos(angles), jnp.sin(angles)], 0))
        other = pltpu.roll(both, 64, 1)
        low = lax.broadcasted_iota(jnp.int32, (PIECE, HEAD), 1) < 64
        values = values_ref[n].astype(jnp.float32)
        return (
            values * jnp.where(low, both, other)
            + pltpu.roll(values, 64, 1) * jnp.where(low, -other, both)
        ).astype(jnp.bfloat16)

    own_q = turn(0)
    own_k = turn(1)
    marks = mask_ref[...].astype(jnp.float32)
    marks = jnp.concatenate([marks, jnp.zeros((4, 112), jnp.float32)], 1)
    marks = jnp.concatenate([marks, jnp.zeros((12, HEAD), jnp.float32)], 0).astype(jnp.bfloat16)
    q_out[:PIECE] = own_q
    q_out[PIECE:] = marks
    for n in range(8):
        k_out[n] = own_k


def early_kernel(after, wq_ref, wk_ref, wq_out, wk_out):
    wq_out[...] = turned(wq_ref[...])
    wk_out[...] = turned(wk_ref[...])


def features(weight_t, rows):
    mapped = nt(weight_t, rows)
    up = jnp.exp(mapped - jnp.max(mapped, 0, keepdims=True))
    down = jnp.exp(jnp.min(mapped, 0, keepdims=True) - mapped)
    up = up * (1.0 / jnp.sum(up, 0, keepdims=True))
    down = down * (1.0 / jnp.sum(down, 0, keepdims=True))
    return jnp.concatenate([up, down], axis=0)


def turned(a):
    return jnp.transpose(a.astype(jnp.float32)).astype(jnp.bfloat16)


def not_after():
    shape = (TILE, TILE)
    return lax.broadcasted_iota(jnp.int32, shape, 0) <= lax.broadcasted_iota(jnp.int32, shape, 1)


def listed(marks, chunks, offset, full, corner):
    x, y, z, c = place()
    counts = [jnp.int32(0), jnp.int32(0)]
    for n, chunk in enumerate(chunks):
        first_tile = ((x + 4 - chunk) % 4) * 32 + c * 16 + y * 4
        for stripe in range(4):
            row_tile = stripe * 32 + z * 4 + x
            back = (y + 4 - stripe) % 4
            row = (back ^ (back // 2)) * 8 + x
            for sub in range(4):
                live = marks[n, row, y * 4 + sub] > 0
                kinds = (first_tile + sub < row_tile, first_tile + sub == row_tile)
                for which, (kind, tiles) in enumerate(zip(kinds, (full, corner))):
                    tiles[counts[which]] = (offset + n * 4 + sub) * 4 + stripe
                    counts[which] = counts[which] + (live & kind).astype(jnp.int32)
    for count, tiles in zip(counts, (full, corner)):
        for n in range(3):
            tiles[count + n] = SPARE
        tiles[LISTED - 1] = count


def in_groups(tiles, width, begin, finish):
    def group(n, ahead):
        here = [tiles[width * n + step] for step in range(width + 1)]
        for step in range(width):
            later = begin(here[step + 1], (step + 1) % width)
            finish(here[step], step, ahead)
            ahead = later
        return ahead

    count = tiles[LISTED - 1]
    lax.fori_loop(0, (count + width - 1) // width, group, begin(tiles[0], 0))


def first_kernel(chunks, *refs):
    count = len(chunks)
    opens, closes = 0 in chunks, 2 in chunks
    offset = 4 * CHUNKS.index(chunks[0])
    refs = list(refs)
    take = lambda number: [refs.pop(0) for _ in range(number)]
    k_refs = take(count + closes)
    (wk_ref,) = take(1)
    if opens:
        wq_ref, *q_refs = take(5)
    else:
        old_run, q_turned, qf_low = take(3)
        take(4)
    run, u_ref, kfeat_ref, kft_ref, keys_ref, full, corner = take(7)
    if opens:
        q_turned, qf_low, qfeat_ref, rows_ref, dk_ref, dq_ref = take(6)
    if closes:
        (stats_ref,) = take(1)
    raw_a, raw_b, kf_ref, staged, marks, sems = refs
    scale = LOG2E * HEAD**-0.5
    x, y, z, c = place()
    fetched = []
    for n in range(count):
        staged[n] = k_refs[n][MARK_ROW : MARK_ROW + MARKS, :].astype(jnp.float32).astype(jnp.int32)
        fetched.append(pltpu.make_async_copy(staged.at[n], marks.at[n], sems.at[n]))
        fetched[-1].start()
    wk_t = wk_ref[...]
    if opens:
        wq_t = wq_ref[...]
        for n, q_ref in enumerate(q_refs):
            stripe = (y + 4 - CHUNKS[n]) % 4
            rows_ref[stripe, c] = q_ref[0, :PIECE]
            rows_ref[stripe, 1 - c] = q_ref[1, :PIECE]
        for stripe in range(4):
            rows = rows_ref[stripe].reshape(TILE, HEAD)
            q_turned[stripe] = turned(rows)
            feat = features(wq_t, rows)
            qfeat_ref[stripe] = feat
            qf_low[stripe] = feat.astype(jnp.bfloat16)
        dk_ref[...] = jnp.zeros_like(dk_ref)
        dq_ref[...] = jnp.zeros_like(dq_ref)
        run[0] = jnp.full((5, 8, TILE), LOW, jnp.float32)
        for n in (1, 2, 3):
            run[n] = jnp.zeros((5, 8, TILE), jnp.float32)
    else:
        run[...] = old_run[...]

    for n in range(count):
        for sub in range(4):
            if closes and chunks[n] == 2 and sub >= 2:
                keys = k_refs[n + 1][(sub - 2) * TILE : (sub - 1) * TILE, :]
            else:
                start = sub * TILE + (MARKS if sub >= 2 else 0)
                keys = k_refs[n][start : start + TILE, :]
            spot = offset + n * 4 + sub
            keys_ref[spot] = keys
            feat = features(wk_t, keys)
            kfeat_ref[spot] = feat
            low = feat.astype(jnp.bfloat16)
            kft_ref[spot] = low
            kf_ref[spot] = jnp.transpose(low)
    for copy in fetched:
        copy.wait()
    listed(marks, chunks, offset, full, corner)

    def begin(tile, side, cut=False):
        raw = nn(keys_ref[tile // 4], q_turned[tile % 4])
        if cut:
            raw = jnp.where(not_after(), raw, LOW)
        (raw_b if side else raw_a)[...] = raw
        top = jnp.max(jnp.max(fold(raw), 0), 0, keepdims=True) * scale
        return jnp.broadcast_to(top, (8, TILE))

    def finish(tile, side, top, cut=False):
        student = nn(kf_ref[tile // 4], qf_low[tile % 4])
        if cut:
            norm = jnp.sum(fold(jnp.where(not_after(), student, 0.0)), 0)
            student = jnp.where(not_after(), student, 1.0)
        else:
            norm = jnp.sum(fold(student), 0)
        score = fold((raw_b if side else raw_a)[...]) * scale
        t = score - top[None]
        weight = jnp.exp2(t)
        log_student = jnp.log2(fold(student))
        u_ref[tile] = (score - log_student).reshape(TILE, TILE)
        total = jnp.sum(weight, 0)
        logs = jnp.sum(weight * log_student, 0)
        stripe = jnp.where(tile == SPARE, 4, tile % 4)
        old = run[0, stripe]
        new = jnp.maximum(old, top)
        left = jnp.exp2(old - new)
        right = jnp.exp2(top - new)
        run[0, stripe] = new
        run[1, stripe] = run[1, stripe] * left + total * right
        run[2, stripe] = run[2, stripe] * left + logs * right
        run[3, stripe] = run[3, stripe] + norm

    in_groups(full, 2, begin, finish)

    def corner_step(n, carry):
        tile = corner[n]
        finish(tile, 0, begin(tile, 0, True), True)
        return carry

    lax.fori_loop(0, corner[LISTED - 1], corner_step, 0)

    if closes:
        lines = [run[0, stripe][:1] for stripe in range(4)] + [
            jnp.sum(run[n, stripe], 0, keepdims=True) for n in (1, 2, 3) for stripe in range(4)
        ]
        lines = jnp.concatenate(lines, 0)
        for copy in range(8):
            stats_ref[copy] = lines


def split2(a):
    high = a.astype(jnp.bfloat16)
    low = (a - high.astype(jnp.float32)).astype(jnp.bfloat16)
    return jnp.concatenate([high, low], axis=0)


def weight_grad(feat, dfeat, rows):
    up, down = feat[:HEAD], feat[HEAD:]
    d1, d2 = dfeat[:HEAD], dfeat[HEAD:]
    dmapped = up * (d1 - jnp.sum(up * d1, 0, keepdims=True)) - down * (
        d2 - jnp.sum(down * d2, 0, keepdims=True)
    )
    parts = nn(split2(dmapped), rows)
    return parts[HEAD:] + parts[:HEAD]


def second_kernel(st_ref, q_ref, qfeat_ref, qf_low, dk_in, dq_in, *refs):
    refs = list(refs)
    u_ref, kfeat_ref, kft_ref, keys_ref = (refs.pop(0) for _ in range(4))
    lists = [[refs.pop(0) for _ in range(2)] for _ in GROUPS]
    loss_ref, grad_ref, dk_ref, dq_ref, lines, losses, g_ref, merged = refs
    count = jnp.int32(0)
    for chunks, (full, _) in zip(GROUPS, lists):
        for n in range(16 * len(chunks)):
            merged[count + n] = full[n]
        count = count + full[LISTED - 1]
    for n in range(WIDTH + 1):
        merged[count + n] = SPARE
    merged[LISTED - 1] = count
    x, y, z, c = place()
    top = st_ref[0, 0:4]
    for n in range(1, 8):
        top = jnp.maximum(top, st_ref[n, 0:4])
    total = jnp.zeros_like(top)
    logs = jnp.zeros_like(top)
    norm = jnp.zeros_like(top)
    for n in range(8):
        factor = jnp.exp2(st_ref[n, 0:4] - top)
        total = total + st_ref[n, 4:8] * factor
        logs = logs + st_ref[n, 8:12] * factor
        norm = norm + st_ref[n, 12:16]
    loss = jnp.log(norm) - (logs / total) * LN2
    for stripe in range(4):
        for half in range(2):
            losses[half, stripe] = jnp.broadcast_to(
                loss[stripe : stripe + 1, half * 128 : half * 128 + 128], (8, 128)
            )
    loss_ref[...] = losses[c, y][:1]
    base = (1.0 / norm) * (1.0 / 32768.0)
    shift = top + jnp.log2(total) + 15.0
    for stripe in range(4):
        lines[0, stripe] = jnp.broadcast_to(base[stripe : stripe + 1], (8, TILE))
        lines[1, stripe] = jnp.broadcast_to(shift[stripe : stripe + 1], (8, TILE))

    def begin(tile, side, cut=False):
        stripe = tile % 4
        grad = lines[0, stripe][None] - jnp.exp2(fold(u_ref[tile]) - lines[1, stripe][None])
        grad = grad.reshape(TILE, TILE)
        if cut:
            grad = jnp.where(not_after(), grad, 0.0)
        g_ref[side] = grad.astype(jnp.bfloat16)
        return 0

    def finish(tile, side, ahead):
        grad = g_ref[side]
        stripe = jnp.where(tile == SPARE, 4, tile % 4)
        dq_ref[stripe] += nn(kft_ref[tile // 4], grad)
        dk_ref[tile // 4] += nt(qf_low[tile % 4], grad)

    in_groups(merged, WIDTH, begin, finish)

    def corner_step(corner, n, carry):
        tile = corner[n]
        begin(tile, 0, True)
        finish(tile, 0, 0)
        return carry

    for _, corner in lists:
        lax.fori_loop(0, corner[LISTED - 1], functools.partial(corner_step, corner), 0)
    gk = jnp.zeros((HEAD, HEAD), jnp.float32)
    for key_tile in range(16):
        gk = gk + weight_grad(kfeat_ref[key_tile], dk_ref[key_tile], keys_ref[key_tile])
    gq = jnp.zeros((HEAD, HEAD), jnp.float32)
    for stripe in range(4):
        gq = gq + weight_grad(
            qfeat_ref[stripe], dq_ref[stripe], q_ref[stripe].reshape(TILE, HEAD)
        )
    grad_ref[0] = jnp.transpose(gq)
    grad_ref[1] = jnp.transpose(gk)


def f32(*shape):
    return jax.ShapeDtypeStruct(shape, jnp.float32)


def b16(*shape):
    return jax.ShapeDtypeStruct(shape, jnp.bfloat16)


def params(work, limit=12):
    return dict(
        compiler_params=pltpu.CompilerParams(vmem_limit_bytes=limit << 20),
        cost_estimate=pl.CostEstimate(
            flops=int(work * 1e8), bytes_accessed=int(work * 1e5), transcendentals=int(work * 1e5)
        ),
    )


VMEM = pl.BlockSpec(memory_space=pltpu.VMEM)
SMEM = pl.BlockSpec(memory_space=pltpu.SMEM)


def first_call(chunks, loads, w_key, *others):
    count = len(chunks)
    outs = [
        f32(4, 5, 8, TILE),
        f32(SPARE + 1, TILE, TILE),
        f32(16, FEAT, TILE),
        b16(17, FEAT, TILE),
        b16(17, TILE, HEAD),
        jax.ShapeDtypeStruct((LISTED,), jnp.int32),
        jax.ShapeDtypeStruct((LISTED,), jnp.int32),
    ]
    if 0 in chunks:
        outs += [
            b16(4, HEAD, TILE),
            b16(4, FEAT, TILE),
            f32(4, FEAT, TILE),
            b16(4, 2, PIECE, HEAD),
            f32(17, FEAT, TILE),
            f32(5, FEAT, TILE),
        ]
    if 2 in chunks:
        outs += [f32(8, 16, TILE)]
    return pl.pallas_call(
        functools.partial(first_kernel, chunks),
        out_shape=tuple(outs),
        in_specs=[VMEM] * (len(loads) + 1 + len(others)),
        out_specs=tuple(SMEM if n in (5, 6) else VMEM for n in range(len(outs))),
        scratch_shapes=[
            pltpu.VMEM((TILE, TILE), jnp.float32),
            pltpu.VMEM((TILE, TILE), jnp.float32),
            pltpu.VMEM((17, TILE, FEAT), jnp.bfloat16),
            pltpu.VMEM((count, MARKS, HEAD), jnp.int32),
            pltpu.SMEM((count, MARKS, HEAD), jnp.int32),
            pltpu.SemaphoreType.DMA((count,)),
        ],
        input_output_aliases={} if 0 in chunks else {len(loads) + 4 + n: 1 + n for n in range(4)},
        name="first%d" % chunks[0],
        **params(20 * count),
    )(*loads, w_key, *others)


def exchanged(copies, axes):
    return lax.all_to_all(copies, axes, split_axis=0, concat_axis=0, tiled=True)


def local(queries, keys, positions, tile_mask, w_query, w_key):
    hbm = pl.BlockSpec(memory_space=pltpu.HBM)
    vmem = pl.BlockSpec(memory_space=pltpu.VMEM)
    q_own, k_copies = pl.pallas_call(
        rotate_kernel,
        out_shape=(b16(PIECE + 16, HEAD), b16(8, PIECE, HEAD)),
        in_specs=[hbm] * 4,
        out_specs=(vmem,) * 2,
        scratch_shapes=[
            pltpu.VMEM((2, 8, PIECE), jnp.int32),
            pltpu.VMEM((2, PIECE, HEAD), jnp.bfloat16),
            pltpu.VMEM((4, 16), jnp.int32),
            pltpu.SemaphoreType.DMA((5,)),
        ],
        compiler_params=pltpu.CompilerParams(vmem_limit_bytes=60 << 20),
        name="rotate",
    )(
        positions.reshape(32, 8, PIECE),
        queries.reshape(PIECE, HEAD),
        keys.reshape(PIECE, HEAD),
        tile_mask,
    )
    k_near = exchanged(k_copies, "z").reshape(4 * TILE, HEAD)
    other = lax.ppermute(q_own, "c", [(0, 1), (1, 0)])
    w_query, w_key = pl.pallas_call(
        early_kernel,
        out_shape=(b16(HEAD, HEAD), b16(HEAD, HEAD)),
        in_specs=[VMEM] * 3,
        out_specs=(VMEM,) * 2,
        name="early",
        **params(10),
    )(other, w_query[0], w_key[0])
    pair = jnp.stack([q_own, other])
    pairs = [pair] + [
        lax.ppermute(pair, "y", [(i, (i + step) % 4) for i in range(4)]) for step in (1, 3, 2)
    ]
    marks = jnp.stack([near[:, PIECE : PIECE + 4] for near in pairs]).reshape(MARKS, HEAD)
    marks, w_query, w_key = lax.optimization_barrier((marks, w_query, w_key))
    half = 2 * TILE
    load = jnp.concatenate([k_near[:half], marks, k_near[half:]], 0)
    after = [(i, (i + 1) % 4) for i in range(4)]
    before = [(i, (i + 3) % 4) for i in range(4)]
    lower = lax.ppermute(load, "x", after)
    upper = lax.ppermute(load, "x", before)
    far = (
        lax.ppermute(lower[: half + MARKS], "x", after),
        lax.ppermute(upper[half + MARKS :], "x", before),
    )
    run, *kept, full0, corner0, q_turned, qf_low, qfeat, q_rows, dk, dq = first_call(
        (0,), [load], w_key, w_query, *pairs
    )
    run, *kept, full1, corner1 = first_call(
        (1, 3), [lower, upper], w_key, run, q_turned, qf_low, *kept
    )
    run, *kept, full2, corner2, stats = first_call(
        (2,), far, w_key, run, q_turned, qf_low, *kept
    )
    stats = exchanged(stats, ("y", "c"))
    loss, grads, _, _ = pl.pallas_call(
        second_kernel,
        out_shape=(f32(1, PIECE), f32(2, HEAD, HEAD), f32(17, FEAT, TILE), f32(5, FEAT, TILE)),
        in_specs=[VMEM] * 10 + [SMEM] * 6,
        out_specs=(VMEM,) * 4,
        scratch_shapes=[
            pltpu.VMEM((2, 4, 8, TILE), jnp.float32),
            pltpu.VMEM((2, 4, 8, 128), jnp.float32),
            pltpu.VMEM((WIDTH, TILE, TILE), jnp.bfloat16),
            pltpu.SMEM((LISTED,), jnp.int32),
        ],
        input_output_aliases={4: 2, 5: 3},
        name="second",
        **params(100),
    )(stats, q_rows, qfeat, qf_low, dk, dq, *kept, full0, corner0, full1, corner1, full2, corner2)
    wide = ("y", "x", "c")
    part = exchanged(grads.reshape(32, 8, HEAD), wide).sum(0)
    part = exchanged(jnp.broadcast_to(part, (8, 8, HEAD)), "z").sum(0)
    whole = exchanged(jnp.broadcast_to(part, (32, 8, HEAD)), wide).reshape(2, 1, HEAD, HEAD)
    return loss.reshape(1, 1, PIECE), whole[0], whole[1]


def solution(mesh):
    finer = Mesh(mesh.devices.reshape(4, 8, 4, 2), ("y", "z", "x", "c"))
    qb, kb = ("y", "z"), ("x", "c")
    placed = (P(qb, kb, None, None), P(kb, qb, None, None), P(), P(qb, kb), P(), P())
    return jax.shard_map(
        local, mesh=finer, in_specs=placed, out_specs=(P(qb, kb, None), P(), P()), check_vma=False
    )
```

```python
import functools

import jax
import jax.numpy as jnp
from jax import lax
from jax.experimental import pallas as pl
from jax.experimental.pallas import tpu as pltpu
from jax.sharding import Mesh
from jax.sharding import PartitionSpec as P

LOW = -1e30
LOG2E = 1.4426950408889634
LN2 = 0.6931471805599453
TILE = 256
HEAD = 128
FEAT = 256
PIECE = 128
MARK_ROW = 512
LISTED = 96
SPARE = 64
WIDTH = 4
GROUPS = ((0,), (1, 3), (2,))
MARKS = 32
CHUNKS = (0, 1, 3, 2)


def nn(a, b):
    return lax.dot_general(a, b, (((1,), (0,)), ((), ())), preferred_element_type=jnp.float32)


def nt(a, b):
    return lax.dot_general(a, b, (((1,), (1,)), ((), ())), preferred_element_type=jnp.float32)


def fold(a):
    return a.reshape(a.shape[0] // 8, 8, a.shape[1])


def place():
    return tuple(lax.axis_index(name) for name in ("x", "y", "z", "c"))


def cosine_and_sine(angles):
    turns = jnp.floor(angles * 0.6366197723675814 + 0.5)
    rest = angles
    for part in (1.5703125, 0.0004825592041015625, 1.2665987014770508e-06, 9.920935184482005e-10):
        rest = rest - turns * jnp.float32(part)
    quarter = turns.astype(jnp.int32)
    z = rest * rest
    sine = rest + rest * z * (
        -1.6666654611e-1 + z * (8.3321608736e-3 + z * -1.9515295891e-4)
    )
    cosine = (1.0 - 0.5 * z) + z * z * (
        4.166664568298827e-2 + z * (-1.388731625493765e-3 + z * 2.443315711809948e-5)
    )
    odd = (quarter & 1) == 1
    first, second = jnp.where(odd, sine, cosine), jnp.where(odd, cosine, sine)
    return (
        jnp.where(((quarter + 1) & 2) == 2, -first, first),
        jnp.where((quarter & 2) == 2, -second, second),
    )


def rotate_kernel(
    pos_hbm, q_hbm, k_hbm, mask_hbm,
    q_out, k_out,
    lines_ref, values_ref, mask_ref, sems,
):
    x, y, z, c = place()
    pieces = ((y * 8 + z) * 8 + x * 2 + c, (x * 2 + c) * 32 + y * 8 + z)
    copies = [
        pltpu.make_async_copy(pos_hbm.at[pieces[0] // 8], lines_ref.at[0], sems.at[0]),
        pltpu.make_async_copy(pos_hbm.at[pieces[1] // 8], lines_ref.at[1], sems.at[1]),
        pltpu.make_async_copy(q_hbm, values_ref.at[0], sems.at[2]),
        pltpu.make_async_copy(k_hbm, values_ref.at[1], sems.at[3]),
        pltpu.make_async_copy(mask_hbm, mask_ref, sems.at[4]),
    ]
    for copy in copies:
        copy.start()
    row = lax.broadcasted_iota(jnp.int32, (8, PIECE), 0)
    base = jnp.ones((8, PIECE), jnp.float32)
    for n in range(1, 8):
        base = jnp.where(row == n, jnp.float32(10000.0 ** (-n / 64)), base)
    frequency = jnp.concatenate(
        [base * jnp.float32(10000.0 ** (-8 * n / 64)) for n in range(8)], 0
    )
    for copy in copies:
        copy.wait()

    def turn(n):
        line = jnp.sum(jnp.where(row == pieces[n] % 8, lines_ref[n], 0), 0, keepdims=True)
        angles = line.astype(jnp.float32) * frequency
        both = jnp.transpose(jnp.concatenate(cosine_and_sine(angles), 0))
        other = pltpu.roll(both, 64, 1)
        low = lax.broadcasted_iota(jnp.int32, (PIECE, HEAD), 1) < 64
        values = values_ref[n].astype(jnp.float32)
        return (
            values * jnp.where(low, both, other)
            + pltpu.roll(values, 64, 1) * jnp.where(low, -other, both)
        ).astype(jnp.bfloat16)

    own_q = turn(0)
    own_k = turn(1)
    marks = mask_ref[...].astype(jnp.float32)
    marks = jnp.concatenate([marks, jnp.zeros((4, 112), jnp.float32)], 1)
    marks = jnp.concatenate([marks, jnp.zeros((12, HEAD), jnp.float32)], 0).astype(jnp.bfloat16)
    q_out[:PIECE] = own_q
    q_out[PIECE:] = marks
    for n in range(8):
        k_out[n] = own_k


def early_kernel(after, wq_ref, wk_ref, wq_out, wk_out):
    wq_out[...] = turned(wq_ref[...])
    wk_out[...] = turned(wk_ref[...])


def features(weight_t, rows):
    mapped = nt(weight_t, rows)
    up = jnp.exp(mapped - jnp.max(mapped, 0, keepdims=True))
    down = jnp.exp(jnp.min(mapped, 0, keepdims=True) - mapped)
    up = up * (1.0 / jnp.sum(up, 0, keepdims=True))
    down = down * (1.0 / jnp.sum(down, 0, keepdims=True))
    return jnp.concatenate([up, down], axis=0)


def turned(a):
    return jnp.transpose(a.astype(jnp.float32)).astype(jnp.bfloat16)


def not_after():
    shape = (TILE, TILE)
    return lax.broadcasted_iota(jnp.int32, shape, 0) <= lax.broadcasted_iota(jnp.int32, shape, 1)


def listed(marks, chunks, offset, full, corner):
    x, y, z, c = place()
    counts = [jnp.int32(0), jnp.int32(0)]
    for n, chunk in enumerate(chunks):
        first_tile = ((x + 4 - chunk) % 4) * 32 + c * 16 + y * 4
        for stripe in range(4):
            row_tile = stripe * 32 + z * 4 + x
            back = (y + 4 - stripe) % 4
            row = (back ^ (back // 2)) * 8 + x
            for sub in range(4):
                live = marks[n, row, y * 4 + sub] > 0
                kinds = (first_tile + sub < row_tile, first_tile + sub == row_tile)
                for which, (kind, tiles) in enumerate(zip(kinds, (full, corner))):
                    tiles[counts[which]] = (offset + n * 4 + sub) * 4 + stripe
                    counts[which] = counts[which] + (live & kind).astype(jnp.int32)
    for count, tiles in zip(counts, (full, corner)):
        for n in range(3):
            tiles[count + n] = SPARE
        tiles[LISTED - 1] = count


def in_groups(tiles, width, begin, finish):
    def group(n, ahead):
        here = [tiles[width * n + step] for step in range(width + 1)]
        for step in range(width):
            later = begin(here[step + 1], (step + 1) % width)
            finish(here[step], step, ahead)
            ahead = later
        return ahead

    count = tiles[LISTED - 1]
    lax.fori_loop(0, (count + width - 1) // width, group, begin(tiles[0], 0))


def first_kernel(chunks, *refs):
    count = len(chunks)
    opens, closes = 0 in chunks, 2 in chunks
    offset = 4 * CHUNKS.index(chunks[0])
    refs = list(refs)
    take = lambda number: [refs.pop(0) for _ in range(number)]
    k_refs = take(count + closes)
    (wk_ref,) = take(1)
    if opens:
        wq_ref, *q_refs = take(5)
    else:
        old_run, q_turned, qf_low = take(3)
        take(5)
    run, u_ref, kfeat_ref, kft_ref, keys_ref, top_ref, full, corner = take(8)
    if opens:
        q_turned, qf_low, qfeat_ref, rows_ref, dk_ref, dq_ref = take(6)
    if closes:
        (stats_ref,) = take(1)
    raw_a, raw_b, kf_ref, staged, marks, sems = refs
    scale = LOG2E * HEAD**-0.5
    x, y, z, c = place()
    fetched = []
    for n in range(count):
        staged[n] = k_refs[n][MARK_ROW : MARK_ROW + MARKS, :].astype(jnp.float32).astype(jnp.int32)
        fetched.append(pltpu.make_async_copy(staged.at[n], marks.at[n], sems.at[n]))
        fetched[-1].start()
    wk_t = wk_ref[...]
    if opens:
        wq_t = wq_ref[...]
        for n, q_ref in enumerate(q_refs):
            stripe = (y + 4 - CHUNKS[n]) % 4
            rows_ref[stripe, c] = q_ref[0, :PIECE]
            rows_ref[stripe, 1 - c] = q_ref[1, :PIECE]
        for stripe in range(4):
            rows = rows_ref[stripe].reshape(TILE, HEAD)
            q_turned[stripe] = turned(rows)
            feat = features(wq_t, rows)
            qfeat_ref[stripe] = feat
            qf_low[stripe] = feat.astype(jnp.bfloat16)
        dk_ref[...] = jnp.zeros_like(dk_ref)
        dq_ref[...] = jnp.zeros_like(dq_ref)
        run[0] = jnp.full((5, 8, TILE), LOW, jnp.float32)
        for n in (1, 2, 3):
            run[n] = jnp.zeros((5, 8, TILE), jnp.float32)
    else:
        run[...] = old_run[...]

    for n in range(count):
        for sub in range(4):
            if closes and chunks[n] == 2 and sub >= 2:
                keys = k_refs[n + 1][(sub - 2) * TILE : (sub - 1) * TILE, :]
            else:
                start = sub * TILE + (MARKS if sub >= 2 else 0)
                keys = k_refs[n][start : start + TILE, :]
            spot = offset + n * 4 + sub
            keys_ref[spot] = keys
            feat = features(wk_t, keys)
            kfeat_ref[spot] = feat
            low = feat.astype(jnp.bfloat16)
            kft_ref[spot] = low
            kf_ref[spot] = jnp.transpose(low)
    for copy in fetched:
        copy.wait()
    listed(marks, chunks, offset, full, corner)

    def begin(tile, side, cut=False):
        raw = nn(keys_ref[tile // 4], q_turned[tile % 4])
        if cut:
            raw = jnp.where(not_after(), raw, LOW)
        (raw_b if side else raw_a)[...] = raw
        top = jnp.max(jnp.max(fold(raw), 0), 0, keepdims=True) * scale
        return jnp.broadcast_to(top, (8, TILE))

    def finish(tile, side, top, cut=False):
        student = nn(kf_ref[tile // 4], qf_low[tile % 4])
        if cut:
            norm = jnp.sum(fold(jnp.where(not_after(), student, 0.0)), 0)
            student = jnp.where(not_after(), student, 1.0)
        else:
            norm = jnp.sum(fold(student), 0)
        t = fold((raw_b if side else raw_a)[...]) * scale - top[None]
        weight = jnp.exp2(t)
        log_student = jnp.log2(fold(student))
        u_ref[tile] = (t - log_student).reshape(TILE, TILE)
        top_ref[tile] = top
        total = jnp.sum(weight, 0)
        logs = jnp.sum(weight * log_student, 0)
        stripe = jnp.where(tile == SPARE, 4, tile % 4)
        old = run[0, stripe]
        new = jnp.maximum(old, top)
        left = jnp.exp2(old - new)
        right = jnp.exp2(top - new)
        run[0, stripe] = new
        run[1, stripe] = run[1, stripe] * left + total * right
        run[2, stripe] = run[2, stripe] * left + logs * right
        run[3, stripe] = run[3, stripe] + norm

    in_groups(full, 2, begin, finish)

    def corner_step(n, carry):
        tile = corner[n]
        finish(tile, 0, begin(tile, 0, True), True)
        return carry

    lax.fori_loop(0, corner[LISTED - 1], corner_step, 0)

    if closes:
        lines = [run[0, stripe][:1] for stripe in range(4)] + [
            jnp.sum(run[n, stripe], 0, keepdims=True) for n in (1, 2, 3) for stripe in range(4)
        ]
        lines = jnp.concatenate(lines, 0)
        for copy in range(8):
            stats_ref[copy] = lines


def split2(a):
    high = a.astype(jnp.bfloat16)
    low = (a - high.astype(jnp.float32)).astype(jnp.bfloat16)
    return jnp.concatenate([high, low], axis=0)


def weight_grad(feat, dfeat, rows):
    up, down = feat[:HEAD], feat[HEAD:]
    d1, d2 = dfeat[:HEAD], dfeat[HEAD:]
    dmapped = up * (d1 - jnp.sum(up * d1, 0, keepdims=True)) - down * (
        d2 - jnp.sum(down * d2, 0, keepdims=True)
    )
    parts = nn(split2(dmapped), rows)
    return parts[HEAD:] + parts[:HEAD]


def second_kernel(st_ref, q_ref, qfeat_ref, qf_low, dk_in, dq_in, *refs):
    refs = list(refs)
    u_ref, kfeat_ref, kft_ref, keys_ref, top_ref = (refs.pop(0) for _ in range(5))
    lists = [[refs.pop(0) for _ in range(2)] for _ in GROUPS]
    loss_ref, grad_ref, dk_ref, dq_ref, lines, losses, g_ref, merged = refs
    count = jnp.int32(0)
    for chunks, (full, _) in zip(GROUPS, lists):
        for n in range(16 * len(chunks)):
            merged[count + n] = full[n]
        count = count + full[LISTED - 1]
    for n in range(WIDTH + 1):
        merged[count + n] = SPARE
    merged[LISTED - 1] = count
    x, y, z, c = place()
    top = st_ref[0, 0:4]
    for n in range(1, 8):
        top = jnp.maximum(top, st_ref[n, 0:4])
    total = jnp.zeros_like(top)
    logs = jnp.zeros_like(top)
    norm = jnp.zeros_like(top)
    for n in range(8):
        factor = jnp.exp2(st_ref[n, 0:4] - top)
        total = total + st_ref[n, 4:8] * factor
        logs = logs + st_ref[n, 8:12] * factor
        norm = norm + st_ref[n, 12:16]
    loss = jnp.log(norm) - (logs / total) * LN2
    for stripe in range(4):
        for half in range(2):
            losses[half, stripe] = jnp.broadcast_to(
                loss[stripe : stripe + 1, half * 128 : half * 128 + 128], (8, 128)
            )
    loss_ref[...] = losses[c, y][:1]
    base = (1.0 / norm) * (1.0 / 32768.0)
    shift = top + jnp.log2(total) + 15.0
    for stripe in range(4):
        lines[0, stripe] = jnp.broadcast_to(base[stripe : stripe + 1], (8, TILE))
        lines[1, stripe] = jnp.broadcast_to(shift[stripe : stripe + 1], (8, TILE))

    def begin(tile, side, cut=False):
        stripe = tile % 4
        less = lines[1, stripe] - top_ref[tile]
        grad = lines[0, stripe][None] - jnp.exp2(fold(u_ref[tile]) - less[None])
        grad = grad.reshape(TILE, TILE)
        if cut:
            grad = jnp.where(not_after(), grad, 0.0)
        g_ref[side] = grad.astype(jnp.bfloat16)
        return 0

    def finish(tile, side, ahead):
        grad = g_ref[side]
        stripe = jnp.where(tile == SPARE, 4, tile % 4)
        dq_ref[stripe] += nn(kft_ref[tile // 4], grad)
        dk_ref[tile // 4] += nt(qf_low[tile % 4], grad)

    in_groups(merged, WIDTH, begin, finish)

    def corner_step(corner, n, carry):
        tile = corner[n]
        begin(tile, 0, True)
        finish(tile, 0, 0)
        return carry

    for _, corner in lists:
        lax.fori_loop(0, corner[LISTED - 1], functools.partial(corner_step, corner), 0)
    gk = jnp.zeros((HEAD, HEAD), jnp.float32)
    for key_tile in range(16):
        gk = gk + weight_grad(kfeat_ref[key_tile], dk_ref[key_tile], keys_ref[key_tile])
    gq = jnp.zeros((HEAD, HEAD), jnp.float32)
    for stripe in range(4):
        gq = gq + weight_grad(
            qfeat_ref[stripe], dq_ref[stripe], q_ref[stripe].reshape(TILE, HEAD)
        )
    grad_ref[0] = jnp.transpose(gq)
    grad_ref[1] = jnp.transpose(gk)


def f32(*shape):
    return jax.ShapeDtypeStruct(shape, jnp.float32)


def b16(*shape):
    return jax.ShapeDtypeStruct(shape, jnp.bfloat16)


def params(work, limit=12):
    return dict(
        compiler_params=pltpu.CompilerParams(vmem_limit_bytes=limit << 20),
        cost_estimate=pl.CostEstimate(
            flops=int(work * 1e8), bytes_accessed=int(work * 1e5), transcendentals=int(work * 1e5)
        ),
    )


VMEM = pl.BlockSpec(memory_space=pltpu.VMEM)
SMEM = pl.BlockSpec(memory_space=pltpu.SMEM)


def first_call(chunks, loads, w_key, *others):
    count = len(chunks)
    outs = [
        f32(4, 5, 8, TILE),
        f32(SPARE + 1, TILE, TILE),
        f32(16, FEAT, TILE),
        b16(17, FEAT, TILE),
        b16(17, TILE, HEAD),
        f32(SPARE + 1, 8, TILE),
        jax.ShapeDtypeStruct((LISTED,), jnp.int32),
        jax.ShapeDtypeStruct((LISTED,), jnp.int32),
    ]
    if 0 in chunks:
        outs += [
            b16(4, HEAD, TILE),
            b16(4, FEAT, TILE),
            f32(4, FEAT, TILE),
            b16(4, 2, PIECE, HEAD),
            f32(17, FEAT, TILE),
            f32(5, FEAT, TILE),
        ]
    if 2 in chunks:
        outs += [f32(8, 16, TILE)]
    return pl.pallas_call(
        functools.partial(first_kernel, chunks),
        out_shape=tuple(outs),
        in_specs=[VMEM] * (len(loads) + 1 + len(others)),
        out_specs=tuple(SMEM if n in (6, 7) else VMEM for n in range(len(outs))),
        scratch_shapes=[
            pltpu.VMEM((TILE, TILE), jnp.float32),
            pltpu.VMEM((TILE, TILE), jnp.float32),
            pltpu.VMEM((17, TILE, FEAT), jnp.bfloat16),
            pltpu.VMEM((count, MARKS, HEAD), jnp.int32),
            pltpu.SMEM((count, MARKS, HEAD), jnp.int32),
            pltpu.SemaphoreType.DMA((count,)),
        ],
        input_output_aliases={} if 0 in chunks else {len(loads) + 4 + n: 1 + n for n in range(5)},
        name="first%d" % chunks[0],
        **params(20 * count),
    )(*loads, w_key, *others)


def exchanged(copies, axes):
    return lax.all_to_all(copies, axes, split_axis=0, concat_axis=0, tiled=True)


def local(queries, keys, positions, tile_mask, w_query, w_key):
    hbm = pl.BlockSpec(memory_space=pltpu.HBM)
    vmem = pl.BlockSpec(memory_space=pltpu.VMEM)
    q_own, k_copies = pl.pallas_call(
        rotate_kernel,
        out_shape=(b16(PIECE + 16, HEAD), b16(8, PIECE, HEAD)),
        in_specs=[hbm] * 4,
        out_specs=(vmem,) * 2,
        scratch_shapes=[
            pltpu.VMEM((2, 8, PIECE), jnp.int32),
            pltpu.VMEM((2, PIECE, HEAD), jnp.bfloat16),
            pltpu.VMEM((4, 16), jnp.int32),
            pltpu.SemaphoreType.DMA((5,)),
        ],
        compiler_params=pltpu.CompilerParams(vmem_limit_bytes=60 << 20),
        name="rotate",
    )(
        positions.reshape(32, 8, PIECE),
        queries.reshape(PIECE, HEAD),
        keys.reshape(PIECE, HEAD),
        tile_mask,
    )
    k_near = exchanged(k_copies, "z").reshape(4 * TILE, HEAD)
    other = lax.ppermute(q_own, "c", [(0, 1), (1, 0)])
    w_query, w_key = pl.pallas_call(
        early_kernel,
        out_shape=(b16(HEAD, HEAD), b16(HEAD, HEAD)),
        in_specs=[VMEM] * 3,
        out_specs=(VMEM,) * 2,
        name="early",
        **params(10),
    )(other, w_query[0], w_key[0])
    pair = jnp.stack([q_own, other])
    pairs = [pair] + [
        lax.ppermute(pair, "y", [(i, (i + step) % 4) for i in range(4)]) for step in (1, 3, 2)
    ]
    marks = jnp.stack([near[:, PIECE : PIECE + 4] for near in pairs]).reshape(MARKS, HEAD)
    marks, w_query, w_key = lax.optimization_barrier((marks, w_query, w_key))
    half = 2 * TILE
    load = jnp.concatenate([k_near[:half], marks, k_near[half:]], 0)
    after = [(i, (i + 1) % 4) for i in range(4)]
    before = [(i, (i + 3) % 4) for i in range(4)]
    lower = lax.ppermute(load, "x", after)
    upper = lax.ppermute(load, "x", before)
    far = (
        lax.ppermute(lower[: half + MARKS], "x", after),
        lax.ppermute(upper[half + MARKS :], "x", before),
    )
    run, *kept, full0, corner0, q_turned, qf_low, qfeat, q_rows, dk, dq = first_call(
        (0,), [load], w_key, w_query, *pairs
    )
    run, *kept, full1, corner1 = first_call(
        (1, 3), [lower, upper], w_key, run, q_turned, qf_low, *kept
    )
    run, *kept, full2, corner2, stats = first_call(
        (2,), far, w_key, run, q_turned, qf_low, *kept
    )
    stats = exchanged(stats, ("y", "c"))
    loss, grads, _, _ = pl.pallas_call(
        second_kernel,
        out_shape=(f32(1, PIECE), f32(2, HEAD, HEAD), f32(17, FEAT, TILE), f32(5, FEAT, TILE)),
        in_specs=[VMEM] * 11 + [SMEM] * 6,
        out_specs=(VMEM,) * 4,
        scratch_shapes=[
            pltpu.VMEM((2, 4, 8, TILE), jnp.float32),
            pltpu.VMEM((2, 4, 8, 128), jnp.float32),
            pltpu.VMEM((WIDTH, TILE, TILE), jnp.bfloat16),
            pltpu.SMEM((LISTED,), jnp.int32),
        ],
        input_output_aliases={4: 2, 5: 3},
        name="second",
        **params(100),
    )(stats, q_rows, qfeat, qf_low, dk, dq, *kept, full0, corner0, full1, corner1, full2, corner2)
    wide = ("y", "x", "c")
    part = exchanged(grads.reshape(32, 8, HEAD), wide).sum(0)
    part = exchanged(jnp.broadcast_to(part, (8, 8, HEAD)), "z").sum(0)
    whole = exchanged(jnp.broadcast_to(part, (32, 8, HEAD)), wide).reshape(2, 1, HEAD, HEAD)
    return loss.reshape(1, 1, PIECE), whole[0], whole[1]


def solution(mesh):
    finer = Mesh(mesh.devices.reshape(4, 8, 4, 2), ("y", "z", "x", "c"))
    qb, kb = ("y", "z"), ("x", "c")
    placed = (P(qb, kb, None, None), P(kb, qb, None, None), P(), P(qb, kb), P(), P())
    return jax.shard_map(
        local, mesh=finer, in_specs=placed, out_specs=(P(qb, kb, None), P(), P()), check_vma=False
    )
```

```python
import functools

import jax
import jax.numpy as jnp
from jax import lax
from jax.experimental import pallas as pl
from jax.experimental.pallas import tpu as pltpu
from jax.sharding import Mesh
from jax.sharding import PartitionSpec as P

LOW = -1e30
LOG2E = 1.4426950408889634
LN2 = 0.6931471805599453
TILE = 256
HEAD = 128
FEAT = 256
PIECE = 128
MARK_ROW = 512
LISTED = 96
SPARE = 64
WIDTH = 4
GROUPS = ((0,), (1, 3), (2,))
MARKS = 32
CHUNKS = (0, 1, 3, 2)


def nn(a, b):
    return lax.dot_general(a, b, (((1,), (0,)), ((), ())), preferred_element_type=jnp.float32)


def nt(a, b):
    return lax.dot_general(a, b, (((1,), (1,)), ((), ())), preferred_element_type=jnp.float32)


def fold(a):
    return a.reshape(a.shape[0] // 8, 8, a.shape[1])


def place():
    return tuple(lax.axis_index(name) for name in ("x", "y", "z", "c"))


def cosine_and_sine(angles):
    turns = jnp.floor(angles * 0.6366197723675814 + 0.5)
    rest = angles
    for part in (1.5703125, 0.0004825592041015625, 1.2665987014770508e-06, 9.920935184482005e-10):
        rest = rest - turns * jnp.float32(part)
    quarter = turns.astype(jnp.int32)
    z = rest * rest
    sine = rest + rest * z * (
        -1.6666654611e-1 + z * (8.3321608736e-3 + z * -1.9515295891e-4)
    )
    cosine = (1.0 - 0.5 * z) + z * z * (
        4.166664568298827e-2 + z * (-1.388731625493765e-3 + z * 2.443315711809948e-5)
    )
    odd = (quarter & 1) == 1
    first, second = jnp.where(odd, sine, cosine), jnp.where(odd, cosine, sine)
    return (
        jnp.where(((quarter + 1) & 2) == 2, -first, first),
        jnp.where((quarter & 2) == 2, -second, second),
    )


def rotate_kernel(
    pos_hbm, q_hbm, k_hbm, mask_hbm,
    q_out, k_out,
    lines_ref, values_ref, mask_ref, sems,
):
    x, y, z, c = place()
    pieces = ((y * 8 + z) * 8 + x * 2 + c, (x * 2 + c) * 32 + y * 8 + z)
    copies = [
        pltpu.make_async_copy(pos_hbm.at[pieces[0] // 8], lines_ref.at[0], sems.at[0]),
        pltpu.make_async_copy(pos_hbm.at[pieces[1] // 8], lines_ref.at[1], sems.at[1]),
        pltpu.make_async_copy(q_hbm, values_ref.at[0], sems.at[2]),
        pltpu.make_async_copy(k_hbm, values_ref.at[1], sems.at[3]),
        pltpu.make_async_copy(mask_hbm, mask_ref, sems.at[4]),
    ]
    for copy in copies:
        copy.start()
    row = lax.broadcasted_iota(jnp.int32, (8, PIECE), 0)
    base = jnp.ones((8, PIECE), jnp.float32)
    for n in range(1, 8):
        base = jnp.where(row == n, jnp.float32(10000.0 ** (-n / 64)), base)
    frequency = jnp.concatenate(
        [base * jnp.float32(10000.0 ** (-8 * n / 64)) for n in range(8)], 0
    )
    for copy in copies:
        copy.wait()

    def turn(n):
        line = jnp.sum(jnp.where(row == pieces[n] % 8, lines_ref[n], 0), 0, keepdims=True)
        angles = line.astype(jnp.float32) * frequency
        both = jnp.transpose(jnp.concatenate(cosine_and_sine(angles), 0))
        other = pltpu.roll(both, 64, 1)
        low = lax.broadcasted_iota(jnp.int32, (PIECE, HEAD), 1) < 64
        values = values_ref[n].astype(jnp.float32)
        return (
            values * jnp.where(low, both, other)
            + pltpu.roll(values, 64, 1) * jnp.where(low, -other, both)
        ).astype(jnp.bfloat16)

    own_q = turn(0)
    own_k = turn(1)
    marks = mask_ref[...].astype(jnp.float32)
    marks = jnp.concatenate([marks, jnp.zeros((4, 112), jnp.float32)], 1)
    marks = jnp.concatenate([marks, jnp.zeros((12, HEAD), jnp.float32)], 0).astype(jnp.bfloat16)
    q_out[:PIECE] = own_q
    q_out[PIECE:] = marks
    for n in range(8):
        k_out[n] = own_k


def early_kernel(after, wq_ref, wk_ref, wq_out, wk_out):
    wq_out[...] = turned(wq_ref[...])
    wk_out[...] = turned(wk_ref[...])


def features(weight_t, rows):
    mapped = nt(weight_t, rows) * LOG2E
    up = jnp.exp2(mapped - jnp.max(mapped, 0, keepdims=True))
    down = jnp.exp2(jnp.min(mapped, 0, keepdims=True) - mapped)
    up = up * (1.0 / jnp.sum(up, 0, keepdims=True))
    down = down * (1.0 / jnp.sum(down, 0, keepdims=True))
    return jnp.concatenate([up, down], axis=0)


def turned(a):
    return jnp.transpose(a.astype(jnp.float32)).astype(jnp.bfloat16)


def not_after():
    shape = (TILE, TILE)
    return lax.broadcasted_iota(jnp.int32, shape, 0) <= lax.broadcasted_iota(jnp.int32, shape, 1)


def listed(marks, chunks, offset, full, corner):
    x, y, z, c = place()
    counts = [jnp.int32(0), jnp.int32(0)]
    for n, chunk in enumerate(chunks):
        first_tile = ((x + 4 - chunk) % 4) * 32 + c * 16 + y * 4
        for stripe in range(4):
            row_tile = stripe * 32 + z * 4 + x
            back = (y + 4 - stripe) % 4
            row = (back ^ (back // 2)) * 8 + x
            for sub in range(4):
                live = marks[n, row, y * 4 + sub] > 0
                kinds = (first_tile + sub < row_tile, first_tile + sub == row_tile)
                for which, (kind, tiles) in enumerate(zip(kinds, (full, corner))):
                    tiles[counts[which]] = (offset + n * 4 + sub) * 4 + stripe
                    counts[which] = counts[which] + (live & kind).astype(jnp.int32)
    for count, tiles in zip(counts, (full, corner)):
        for n in range(3):
            tiles[count + n] = SPARE
        tiles[LISTED - 1] = count


def in_groups(tiles, width, begin, finish):
    def group(n, ahead):
        here = [tiles[width * n + step] for step in range(width + 1)]
        for step in range(width):
            later = begin(here[step + 1], (step + 1) % width)
            finish(here[step], step, ahead)
            ahead = later
        return ahead

    count = tiles[LISTED - 1]
    lax.fori_loop(0, (count + width - 1) // width, group, begin(tiles[0], 0))


def first_kernel(chunks, *refs):
    count = len(chunks)
    opens, closes = 0 in chunks, 2 in chunks
    offset = 4 * CHUNKS.index(chunks[0])
    refs = list(refs)
    take = lambda number: [refs.pop(0) for _ in range(number)]
    k_refs = take(count + closes)
    (wk_ref,) = take(1)
    if opens:
        wq_ref, *q_refs = take(5)
    else:
        old_run, q_turned, qf_low = take(3)
        take(5)
    run, u_ref, kfeat_ref, kft_ref, keys_ref, top_ref, full, corner = take(8)
    if opens:
        q_turned, qf_low, qfeat_ref, rows_ref, dk_ref, dq_ref = take(6)
    if closes:
        (stats_ref,) = take(1)
    raw_a, raw_b, kf_ref, staged, marks, sems = refs
    scale = LOG2E * HEAD**-0.5
    x, y, z, c = place()
    fetched = []
    for n in range(count):
        staged[n] = k_refs[n][MARK_ROW : MARK_ROW + MARKS, :].astype(jnp.float32).astype(jnp.int32)
        fetched.append(pltpu.make_async_copy(staged.at[n], marks.at[n], sems.at[n]))
        fetched[-1].start()
    wk_t = wk_ref[...]
    if opens:
        wq_t = wq_ref[...]
        for n, q_ref in enumerate(q_refs):
            stripe = (y + 4 - CHUNKS[n]) % 4
            rows_ref[stripe, c] = q_ref[0, :PIECE]
            rows_ref[stripe, 1 - c] = q_ref[1, :PIECE]
        for stripe in range(4):
            rows = rows_ref[stripe].reshape(TILE, HEAD)
            q_turned[stripe] = turned(rows)
            feat = features(wq_t, rows)
            qfeat_ref[stripe] = feat
            qf_low[stripe] = feat.astype(jnp.bfloat16)
        dk_ref[...] = jnp.zeros_like(dk_ref)
        dq_ref[...] = jnp.zeros_like(dq_ref)
        run[0] = jnp.full((5, 8, TILE), LOW, jnp.float32)
        for n in (1, 2, 3):
            run[n] = jnp.zeros((5, 8, TILE), jnp.float32)
    else:
        run[...] = old_run[...]

    for n in range(count):
        for sub in range(4):
            if closes and chunks[n] == 2 and sub >= 2:
                keys = k_refs[n + 1][(sub - 2) * TILE : (sub - 1) * TILE, :]
            else:
                start = sub * TILE + (MARKS if sub >= 2 else 0)
                keys = k_refs[n][start : start + TILE, :]
            spot = offset + n * 4 + sub
            keys_ref[spot] = keys
            feat = features(wk_t, keys)
            kfeat_ref[spot] = feat
            low = feat.astype(jnp.bfloat16)
            kft_ref[spot] = low
            kf_ref[spot] = jnp.transpose(low)
    for copy in fetched:
        copy.wait()
    listed(marks, chunks, offset, full, corner)

    def begin(tile, side, cut=False):
        raw = nn(keys_ref[tile // 4], q_turned[tile % 4])
        if cut:
            raw = jnp.where(not_after(), raw, LOW)
        (raw_b if side else raw_a)[...] = raw
        top = jnp.max(jnp.max(fold(raw), 0), 0, keepdims=True) * scale
        return jnp.broadcast_to(top, (8, TILE))

    def finish(tile, side, top, cut=False):
        student = nn(kf_ref[tile // 4], qf_low[tile % 4])
        if cut:
            norm = jnp.sum(fold(jnp.where(not_after(), student, 0.0)), 0)
            student = jnp.where(not_after(), student, 1.0)
        else:
            norm = jnp.sum(fold(student), 0)
        t = fold((raw_b if side else raw_a)[...]) * scale - top[None]
        weight = jnp.exp2(t)
        log_student = jnp.log2(fold(student))
        u_ref[tile] = (t - log_student).reshape(TILE, TILE)
        top_ref[tile] = top
        total = jnp.sum(weight, 0)
        logs = jnp.sum(weight * log_student, 0)
        stripe = jnp.where(tile == SPARE, 4, tile % 4)
        old = run[0, stripe]
        new = jnp.maximum(old, top)
        left = jnp.exp2(old - new)
        right = jnp.exp2(top - new)
        run[0, stripe] = new
        run[1, stripe] = run[1, stripe] * left + total * right
        run[2, stripe] = run[2, stripe] * left + logs * right
        run[3, stripe] = run[3, stripe] + norm

    in_groups(full, 2, begin, finish)

    def corner_step(n, carry):
        tile = corner[n]
        finish(tile, 0, begin(tile, 0, True), True)
        return carry

    lax.fori_loop(0, corner[LISTED - 1], corner_step, 0)

    if closes:
        lines = [run[0, stripe][:1] for stripe in range(4)] + [
            jnp.sum(run[n, stripe], 0, keepdims=True) for n in (1, 2, 3) for stripe in range(4)
        ]
        lines = jnp.concatenate(lines, 0)
        for copy in range(8):
            stats_ref[copy] = lines


def split2(a):
    high = a.astype(jnp.bfloat16)
    low = (a - high.astype(jnp.float32)).astype(jnp.bfloat16)
    return jnp.concatenate([high, low], axis=0)


def dmapped(feat, dfeat):
    up, down = feat[:HEAD], feat[HEAD:]
    d1, d2 = dfeat[:HEAD], dfeat[HEAD:]
    return split2(
        up * (d1 - jnp.sum(up * d1, 0, keepdims=True))
        - down * (d2 - jnp.sum(down * d2, 0, keepdims=True))
    )


def weight_grad(halves, rows):
    parts = nn(halves, rows)
    return parts[HEAD:] + parts[:HEAD]


def second_kernel(st_ref, q_ref, qfeat_ref, qf_low, dk_in, dq_in, *refs):
    refs = list(refs)
    u_ref, kfeat_ref, kft_ref, keys_ref, top_ref = (refs.pop(0) for _ in range(5))
    lists = [[refs.pop(0) for _ in range(2)] for _ in GROUPS]
    loss_ref, grad_ref, dk_ref, dq_ref, lines, losses, g_ref, merged, halves = refs
    count = jnp.int32(0)
    for chunks, (full, _) in zip(GROUPS, lists):
        for n in range(16 * len(chunks)):
            merged[count + n] = full[n]
        count = count + full[LISTED - 1]
    for n in range(WIDTH + 1):
        merged[count + n] = SPARE
    merged[LISTED - 1] = count
    x, y, z, c = place()
    top = st_ref[0, 0:4]
    for n in range(1, 8):
        top = jnp.maximum(top, st_ref[n, 0:4])
    total = jnp.zeros_like(top)
    logs = jnp.zeros_like(top)
    norm = jnp.zeros_like(top)
    for n in range(8):
        factor = jnp.exp2(st_ref[n, 0:4] - top)
        total = total + st_ref[n, 4:8] * factor
        logs = logs + st_ref[n, 8:12] * factor
        norm = norm + st_ref[n, 12:16]
    loss = jnp.log(norm) - (logs / total) * LN2
    for stripe in range(4):
        for half in range(2):
            losses[half, stripe] = jnp.broadcast_to(
                loss[stripe : stripe + 1, half * 128 : half * 128 + 128], (8, 128)
            )
    loss_ref[...] = losses[c, y][:1]
    base = (1.0 / norm) * (1.0 / 32768.0)
    shift = top + jnp.log2(total) + 15.0
    for stripe in range(4):
        lines[0, stripe] = jnp.broadcast_to(base[stripe : stripe + 1], (8, TILE))
        lines[1, stripe] = jnp.broadcast_to(shift[stripe : stripe + 1], (8, TILE))

    def begin(tile, side, cut=False):
        stripe = tile % 4
        less = lines[1, stripe] - top_ref[tile]
        grad = lines[0, stripe][None] - jnp.exp2(fold(u_ref[tile]) - less[None])
        grad = grad.reshape(TILE, TILE)
        if cut:
            grad = jnp.where(not_after(), grad, 0.0)
        g_ref[side] = grad.astype(jnp.bfloat16)
        return 0

    def finish(tile, side, ahead):
        grad = g_ref[side]
        stripe = jnp.where(tile == SPARE, 4, tile % 4)
        dq_ref[stripe] += nn(kft_ref[tile // 4], grad)
        dk_ref[tile // 4] += nt(qf_low[tile % 4], grad)

    in_groups(merged, WIDTH, begin, finish)

    def corner_step(corner, n, carry):
        tile = corner[n]
        begin(tile, 0, True)
        finish(tile, 0, 0)
        return carry

    for _, corner in lists:
        lax.fori_loop(0, corner[LISTED - 1], functools.partial(corner_step, corner), 0)
    for key_tile in range(16):
        halves[:, key_tile * TILE : (key_tile + 1) * TILE] = dmapped(
            kfeat_ref[key_tile], dk_ref[key_tile]
        )
    gk = weight_grad(halves[...], keys_ref[0:16].reshape(16 * TILE, HEAD))
    for stripe in range(4):
        halves[:, stripe * TILE : (stripe + 1) * TILE] = dmapped(
            qfeat_ref[stripe], dq_ref[stripe]
        )
    gq = weight_grad(halves[:, : 4 * TILE], q_ref[...].reshape(4 * TILE, HEAD))
    grad_ref[0] = jnp.transpose(gq)
    grad_ref[1] = jnp.transpose(gk)


def f32(*shape):
    return jax.ShapeDtypeStruct(shape, jnp.float32)


def b16(*shape):
    return jax.ShapeDtypeStruct(shape, jnp.bfloat16)


def params(work, limit=12, hoist=200):
    return dict(
        compiler_params=pltpu.CompilerParams(
            vmem_limit_bytes=limit << 20,
        ),
        cost_estimate=pl.CostEstimate(
            flops=int(work * 1e8), bytes_accessed=int(work * 1e5), transcendentals=int(work * 1e5)
        ),
    )


VMEM = pl.BlockSpec(memory_space=pltpu.VMEM)
SMEM = pl.BlockSpec(memory_space=pltpu.SMEM)


def first_call(chunks, loads, w_key, *others):
    count = len(chunks)
    outs = [
        f32(4, 5, 8, TILE),
        f32(SPARE + 1, TILE, TILE),
        f32(16, FEAT, TILE),
        b16(17, FEAT, TILE),
        b16(17, TILE, HEAD),
        f32(SPARE + 1, 8, TILE),
        jax.ShapeDtypeStruct((LISTED,), jnp.int32),
        jax.ShapeDtypeStruct((LISTED,), jnp.int32),
    ]
    if 0 in chunks:
        outs += [
            b16(4, HEAD, TILE),
            b16(4, FEAT, TILE),
            f32(4, FEAT, TILE),
            b16(4, 2, PIECE, HEAD),
            f32(17, FEAT, TILE),
            f32(5, FEAT, TILE),
        ]
    if 2 in chunks:
        outs += [f32(8, 16, TILE)]
    return pl.pallas_call(
        functools.partial(first_kernel, chunks),
        out_shape=tuple(outs),
        in_specs=[VMEM] * (len(loads) + 1 + len(others)),
        out_specs=tuple(SMEM if n in (6, 7) else VMEM for n in range(len(outs))),
        scratch_shapes=[
            pltpu.VMEM((TILE, TILE), jnp.float32),
            pltpu.VMEM((TILE, TILE), jnp.float32),
            pltpu.VMEM((17, TILE, FEAT), jnp.bfloat16),
            pltpu.VMEM((count, MARKS, HEAD), jnp.int32),
            pltpu.SMEM((count, MARKS, HEAD), jnp.int32),
            pltpu.SemaphoreType.DMA((count,)),
        ],
        input_output_aliases={} if 0 in chunks else {len(loads) + 4 + n: 1 + n for n in range(5)},
        name="first%d" % chunks[0],
        **params(20 * count),
    )(*loads, w_key, *others)


def exchanged(copies, axes):
    return lax.all_to_all(copies, axes, split_axis=0, concat_axis=0, tiled=True)


def local(queries, keys, positions, tile_mask, w_query, w_key):
    hbm = pl.BlockSpec(memory_space=pltpu.HBM)
    vmem = pl.BlockSpec(memory_space=pltpu.VMEM)
    q_own, k_copies = pl.pallas_call(
        rotate_kernel,
        out_shape=(b16(PIECE + 16, HEAD), b16(8, PIECE, HEAD)),
        in_specs=[hbm] * 4,
        out_specs=(vmem,) * 2,
        scratch_shapes=[
            pltpu.VMEM((2, 8, PIECE), jnp.int32),
            pltpu.VMEM((2, PIECE, HEAD), jnp.bfloat16),
            pltpu.VMEM((4, 16), jnp.int32),
            pltpu.SemaphoreType.DMA((5,)),
        ],
        compiler_params=pltpu.CompilerParams(vmem_limit_bytes=60 << 20),
        name="rotate",
    )(
        positions.reshape(32, 8, PIECE),
        queries.reshape(PIECE, HEAD),
        keys.reshape(PIECE, HEAD),
        tile_mask,
    )
    k_near = exchanged(k_copies, "z").reshape(4 * TILE, HEAD)
    other = lax.ppermute(q_own, "c", [(0, 1), (1, 0)])
    w_query, w_key = pl.pallas_call(
        early_kernel,
        out_shape=(b16(HEAD, HEAD), b16(HEAD, HEAD)),
        in_specs=[VMEM] * 3,
        out_specs=(VMEM,) * 2,
        name="early",
        **params(10),
    )(other, w_query[0], w_key[0])
    pair = jnp.stack([q_own, other])
    pairs = [pair] + [
        lax.ppermute(pair, "y", [(i, (i + step) % 4) for i in range(4)]) for step in (1, 3, 2)
    ]
    marks = jnp.stack([near[:, PIECE : PIECE + 4] for near in pairs]).reshape(MARKS, HEAD)
    marks, w_query, w_key = lax.optimization_barrier((marks, w_query, w_key))
    half = 2 * TILE
    load = jnp.concatenate([k_near[:half], marks, k_near[half:]], 0)
    after = [(i, (i + 1) % 4) for i in range(4)]
    before = [(i, (i + 3) % 4) for i in range(4)]
    lower = lax.ppermute(load, "x", after)
    upper = lax.ppermute(load, "x", before)
    far = (
        lax.ppermute(lower[: half + MARKS], "x", after),
        lax.ppermute(upper[half + MARKS :], "x", before),
    )
    run, *kept, full0, corner0, q_turned, qf_low, qfeat, q_rows, dk, dq = first_call(
        (0,), [load], w_key, w_query, *pairs
    )
    run, *kept, full1, corner1 = first_call(
        (1, 3), [lower, upper], w_key, run, q_turned, qf_low, *kept
    )
    run, *kept, full2, corner2, stats = first_call(
        (2,), far, w_key, run, q_turned, qf_low, *kept
    )
    stats = exchanged(stats, ("y", "c"))
    loss, grads, _, _ = pl.pallas_call(
        second_kernel,
        out_shape=(f32(1, PIECE), f32(2, HEAD, HEAD), f32(17, FEAT, TILE), f32(5, FEAT, TILE)),
        in_specs=[VMEM] * 11 + [SMEM] * 6,
        out_specs=(VMEM,) * 4,
        scratch_shapes=[
            pltpu.VMEM((2, 4, 8, TILE), jnp.float32),
            pltpu.VMEM((2, 4, 8, 128), jnp.float32),
            pltpu.VMEM((WIDTH, TILE, TILE), jnp.bfloat16),
            pltpu.SMEM((LISTED,), jnp.int32),
            pltpu.VMEM((2 * HEAD, 16 * TILE), jnp.bfloat16),
        ],
        input_output_aliases={4: 2, 5: 3},
        name="second",
        **params(100, hoist=600),
    )(stats, q_rows, qfeat, qf_low, dk, dq, *kept, full0, corner0, full1, corner1, full2, corner2)
    wide = ("y", "x", "c")
    part = exchanged(grads.reshape(32, 8, HEAD), wide).sum(0)
    part = exchanged(jnp.broadcast_to(part, (8, 8, HEAD)), "z").sum(0)
    whole = exchanged(jnp.broadcast_to(part, (32, 8, HEAD)), wide).reshape(2, 1, HEAD, HEAD)
    return loss.reshape(1, 1, PIECE), whole[0], whole[1]


def solution(mesh):
    finer = Mesh(mesh.devices.reshape(4, 8, 4, 2), ("y", "z", "x", "c"))
    qb, kb = ("y", "z"), ("x", "c")
    placed = (P(qb, kb, None, None), P(kb, qb, None, None), P(), P(qb, kb), P(), P())
    return jax.shard_map(
        local, mesh=finer, in_specs=placed, out_specs=(P(qb, kb, None), P(), P()), check_vma=False
    )
```
